32 devices in a mesh: grp: 2 (over x), seq: 16 (over z, y, core).
Axes of the slice: x: 2, y: 2, z: 4, core: 2. Of those that a mesh axis runs over, the one named last changes fastest.
Arguments:
- item_features: bfloat16 [4096, 1024], P(('grp', 'seq')), parts along dimension 0, may hold values from -6 to 6
- tower_in: bfloat16 [1024, 2048], replicated, may hold values from -0.1875 to 0.1875
- tower_out: bfloat16 [2048, 512], replicated, may hold values from -0.125 to 0.125
- proj_weight: bfloat16 [512, 2048], replicated, may hold values from -0.25 to 0.25
- out_weight: bfloat16 [512, 512], replicated, may hold values from -0.25 to 0.25
- hist_keys: bfloat16 [4, 16384, 512], P('grp', 'seq'), parts along dimension 0, may hold values from -6 to 6
- hist_values: bfloat16 [4, 16384, 512], P('grp', 'seq'), parts along dimension 0, may hold values from -6 to 6
- owner_of: int32 [512, 2, 1], P(('grp', 'seq')), parts along dimension 0, may hold values from 0 to 15; in each aligned block of 32 rows (0 to 31, 32 to 63, ..., all dimensions but the last counted through in order) at most 4 rows name the same one
- row_in: int32 [512, 2], P(('grp', 'seq')), parts along dimension 0, may hold values from 0 to 127
- hist_lengths: int32 [4], P('grp'), parts along dimension 0, may hold values from 4096 to 16384
- causal_offsets: int32 [512, 2], P('grp'), parts along dimension 0, may hold values from 0 to 1023
Outputs:
- item_embed: bfloat16 [4096, 512], P(('grp', 'seq')), parts along dimension 0
- cand_out: bfloat16 [512, 2, 512], P(('grp', 'seq')), parts along dimension 0
The draws below stay inside these ranges and needn't reach their ends.
There are 2 independent parts, one for each index of `grp`. The reference program is written for one: setup_inputs(seed, part) draws one part's arguments, and reference() takes and returns one part's arrays. A program takes and returns all parts, laid end to end along the dimension named above; an argument that names none is the same for every part. Nothing has to cross between parts.
Inputs may be any that keep to these rules, and one draw needn't show every extreme that they name: `owner_of`: within the 32 slots of one device (candidate-major), no device number appears more than 4 times.
All inputs are finite; a program needn't handle non-finite values.
Results may differ from the reference program's by a relative error of at most 0.011.
Values may be sent and summed in bfloat16 or wider, within the bound.
No kernel may reach another device: no remote copies, remote signals or barrier semaphores. Data moves between devices by JAX's collectives and lax.ppermute only.
A program may use at most 128 MiB of HBM per device.

```python
import math
import jax
import jax.numpy as jnp
import numpy as np
from jax import lax

D = 512
FEAT = 1024
TOWER = 2048
HEADS = 8
USERS = 2
CAND_DEV = 128
CPS_DEV = 16
HIST_DEV = 1024
CAND = 2048
CPS = 256
HIST = 16384
MOST = 4
N_SEQ = 16


def with_ends(drawn, own_key, least, largest):
    longest = drawn.shape.index(max(drawn.shape))
    spots = []
    for shift in (0, 1):
        where = [jax.random.randint(jax.random.fold_in(own_key, axis), (), 0, length) for axis, length in enumerate(drawn.shape)]
        where[longest] = (where[longest] + shift) % drawn.shape[longest]
        spots.append(tuple(where))
    return drawn.at[spots[0]].set(least).at[spots[1]].set(largest)


def block_scale(key, dims, split, low, high):
    gain, own = 1.0, jax.random.fold_in(key, 6)
    for dim, blocks in split:
        draws = jnp.exp(jax.random.uniform(jax.random.fold_in(own, dim), (blocks,), jnp.float32, low / len(split), high / len(split)))
        gain = gain * jnp.repeat(draws, dims[dim] // blocks).reshape([-1 if axis == dim else 1 for axis in range(len(dims))])
    return gain


def assign_block(key, own, number, rows, number_of, top, most, slope):
    order = jax.random.permutation(key, number_of)
    crowded, ordinary = portions_of(number_of, rows * top, most, slope, True), portions_of(number_of, rows * top, most, slope, False)
    places = jnp.arange(number_of)

    def named(lengths, turn):
        used = int((lengths > 0).sum())
        fixed = max(1, used // 4)
        moved = fixed + (places - fixed + turn * (used - fixed)) % max(1, number_of - fixed)
        return jnp.zeros((number_of,), jnp.int32).at[order[jnp.where(places < fixed, places, moved)]].set(jnp.asarray(lengths, jnp.int32))

    lengths = jnp.where(number % 4 == 0, named(crowded, number // 4), named(ordinary, number - number // 4 - 1))
    mixed = jax.random.permutation(jax.random.fold_in(own, 3), number_of)
    giver, receiver = mixed[0:number_of // 2 * 2:2], mixed[1:number_of // 2 * 2:2]
    room = jnp.minimum(lengths[giver] - 1, most - lengths[receiver]) // 2
    room = jnp.where((giver == order[0]) | (receiver == order[0]) | (lengths[receiver] == 0), 0, jnp.maximum(room, 0))
    moved = jax.random.randint(jax.random.fold_in(own, 4), (number_of // 2,), 0, 1 << 20) % (room + 1)
    lengths = lengths.at[giver].add(-moved).at[receiver].add(moved)
    items = jnp.searchsorted(jnp.cumsum(lengths), jnp.arange(rows * top), side="right").astype(jnp.int32)
    grid = items.reshape(top, rows).T
    grid = grid[jax.random.permutation(jax.random.fold_in(own, 1), rows)]
    turn = jax.random.randint(jax.random.fold_in(own, 2), (rows, 1), 0, top)
    return jnp.take_along_axis(grid, (jnp.arange(top)[None, :] + turn) % top, axis=1)


def portions_of(number_of, total, bound, slope, full):
    weights = [(1 << 20) // math.isqrt(standing ** slope) + 1 for standing in range(1, number_of + 1)]
    largest = bound if full else min(bound, max(-(-total // number_of), total * weights[0] // sum(weights)))
    least = 1 if total - largest >= number_of - 1 else 0
    given, spare = [largest] + [least] * (number_of - 1), total - largest - least * (number_of - 1)
    while spare > 0:
        free = [i for i in range(1, number_of) if given[i] < largest] or [i for i in range(1, number_of) if given[i] < bound]
        whole, budget = sum([weights[i] for i in free]), spare
        for i in free:
            more = min(bound - given[i], max(1, budget * weights[i] // whole), spare)
            given[i] = given[i] + more
            spare = spare - more
    return np.array(given)


def centred(key, shape, spread, reach, pieces=(), kind=jnp.bfloat16):
    array = spread * jax.random.normal(key, shape, jnp.float32)
    if pieces:
        array = array * block_scale(key, shape, pieces, -0.22, 0.18)
    return jnp.clip(array, -reach, reach).astype(kind)


def setup_inputs(seed: int = 0, part: int = 0) -> dict:
    key_list = jax.random.split(jax.random.key(seed), 12)
    part_splits = jax.random.split(jax.random.fold_in(key_list[11], part), 12)
    item_features = centred(part_splits[0], (CAND, FEAT), 1.0, 6.0, ((0, 16),))
    tower_in = centred(key_list[1], (FEAT, TOWER), FEAT ** -0.5, 0.1875)
    tower_out = centred(key_list[2], (TOWER, D), TOWER ** -0.5, 0.125)
    proj_weight = centred(key_list[3], (D, 4 * D), D ** -0.5, 0.25)
    out_weight = centred(key_list[4], (D, D), D ** -0.5, 0.25)
    hist_keys = centred(part_splits[5], (USERS, HIST, D), 1.0, 6.0, ((1, 16),))
    hist_values = centred(part_splits[6], (USERS, HIST, D), 1.0, 6.0, ((1, 16),))
    owner_of_keys = jax.random.split(jax.random.fold_in(part_splits[7], 1), CPS * USERS // (CPS_DEV * USERS))
    owner_of_turns = jax.random.permutation(jax.random.fold_in(part_splits[7], 3), CPS * USERS // (CPS_DEV * USERS))
    owner_of = jax.vmap(lambda own, number: assign_block(jax.random.fold_in(part_splits[7], 2), own, number, CPS_DEV * USERS, N_SEQ, 1, MOST, 2))(owner_of_keys, owner_of_turns).reshape((CPS, USERS, 1))
    row_in = with_ends(jax.random.randint(part_splits[8], (CPS, USERS), 0, CAND_DEV), jax.random.fold_in(part_splits[8], 1), 0, CAND_DEV - 1).astype(jnp.int32)
    hist_lengths = jax.random.randint(part_splits[9], (USERS,), HIST // 4, HIST + 1).astype(jnp.int32)
    causal_offsets = with_ends(jax.random.randint(part_splits[10], (CPS, USERS), 0, HIST_DEV), jax.random.fold_in(part_splits[10], 1), 0, HIST_DEV - 1).astype(jnp.int32)
    return dict(item_features=item_features, tower_in=tower_in, tower_out=tower_out, proj_weight=proj_weight, out_weight=out_weight, hist_keys=hist_keys, hist_values=hist_values, owner_of=owner_of, row_in=row_in, hist_lengths=hist_lengths, causal_offsets=causal_offsets)


def layer_norm(values):
    centre = values - lax.optimization_barrier(jnp.mean(values, axis=-1, keepdims=True))
    return centre * lax.rsqrt(lax.optimization_barrier(jnp.mean(centre * centre, axis=-1, keepdims=True)) + 1e-05)

def self_term(query, key, value):
    rows = query.shape[0]
    size = D // HEADS
    q_heads = query.astype(jnp.float32).reshape(rows, HEADS, size)
    k_heads = key.astype(jnp.float32).reshape(rows, HEADS, size)
    v_heads = value.astype(jnp.float32).reshape(rows, HEADS, size)
    score = lax.optimization_barrier(jnp.sum(q_heads * k_heads, axis=-1)) * size ** (-0.5)
    return (jax.nn.silu(score)[:, :, None] * v_heads).reshape(rows, D)

def attend_block(query, keys, values, visible):
    rows = query.shape[0]
    size = D // HEADS
    q_heads = query.astype(jnp.float32).reshape(rows, HEADS, size)
    k_heads = keys.astype(jnp.float32).reshape(keys.shape[0], HEADS, size)
    v_heads = values.astype(jnp.float32).reshape(values.shape[0], HEADS, size)
    scores = jnp.einsum('chd,jhd->hcj', q_heads, k_heads, precision=lax.Precision.HIGHEST) * size ** (-0.5)
    weights = jnp.where(visible[None], jax.nn.silu(scores), 0.0).astype(jnp.bfloat16)
    mixed = jnp.einsum('hcj,jhd->chd', weights.astype(jnp.float32), v_heads, precision=lax.Precision.HIGHEST)
    return mixed.reshape(rows, D)

def user_attention(operands):
    query, keys, values, limit = operands
    key_blocks = keys.reshape(N_SEQ, HIST_DEV, D)
    value_blocks = values.reshape(N_SEQ, HIST_DEV, D)

    def step(total, block):
        index, key_block, value_block = block
        positions = index * HIST_DEV + jnp.arange(HIST_DEV, dtype=jnp.int32)
        visible = positions[None, :] < limit[:, None]
        return (total + attend_block(query, key_block, value_block, visible), None)
    start = jnp.zeros((CPS, D), jnp.float32)
    total, _ = lax.scan(step, start, (jnp.arange(N_SEQ, dtype=jnp.int32), key_blocks, value_blocks))
    return total

def reference(item_features, tower_in, tower_out, proj_weight, out_weight, hist_keys, hist_values, owner_of, row_in, hist_lengths, causal_offsets):
    hidden = jax.nn.silu(jnp.dot(item_features, tower_in, preferred_element_type=jnp.float32)).astype(jnp.bfloat16)
    item_embed = jnp.dot(hidden, tower_out, preferred_element_type=jnp.float32).astype(jnp.bfloat16)
    pool = (owner_of[:, :, 0].astype(jnp.int32) * CAND_DEV + row_in.astype(jnp.int32)).reshape(-1)
    routed = jnp.take(item_embed, pool, axis=0)
    proj = jax.nn.silu(jnp.dot(routed, proj_weight, preferred_element_type=jnp.float32))
    gate = proj[:, :D]
    value = proj[:, D:2 * D].astype(jnp.bfloat16)
    query = proj[:, 2 * D:3 * D].astype(jnp.bfloat16)
    key = proj[:, 3 * D:].astype(jnp.bfloat16)
    own = self_term(query, key, value)
    query_users = query.reshape(CPS, USERS, D).transpose(1, 0, 2)
    limits = (hist_lengths[None, :] - causal_offsets).T
    attended = lax.map(user_attention, (query_users, hist_keys, hist_values, limits))
    total = attended.transpose(1, 0, 2).reshape(CPS * USERS, D) + own
    mixed = (layer_norm(total) * gate).astype(jnp.bfloat16)
    result = routed.astype(jnp.float32) + jnp.dot(mixed, out_weight, preferred_element_type=jnp.float32)
    return (item_embed, result.astype(jnp.bfloat16).reshape(CPS, USERS, D))
```

```python
import functools

import jax
import jax.numpy as jnp
from jax import lax
from jax.experimental import pallas as pl
from jax.experimental.pallas import tpu as pltpu
from jax.sharding import PartitionSpec as P

HEADS = 8
LANES = 128


def layer_norm(values):
    centre = values - jnp.mean(values, axis=-1, keepdims=True)
    return centre * lax.rsqrt(jnp.mean(centre * centre, axis=-1, keepdims=True) + 1e-05)


def self_term(query, key, value):
    rows, width = query.shape
    size = width // HEADS
    q_heads = query.astype(jnp.float32).reshape(rows, HEADS, size)
    k_heads = key.astype(jnp.float32).reshape(rows, HEADS, size)
    v_heads = value.astype(jnp.float32).reshape(rows, HEADS, size)
    score = jnp.sum(q_heads * k_heads, axis=-1) * size ** (-0.5)
    return (jax.nn.silu(score)[:, :, None] * v_heads).reshape(rows, width)


def attend_kernel(routed_ref, weight_ref, first_ref, second_ref, keys_a, values_a, keys_b, values_b, out_ref):
    rows, width = routed_ref.shape
    size = width // HEADS
    query = jax.nn.silu(
        jnp.dot(routed_ref[...], weight_ref[...], preferred_element_type=jnp.float32)
    ).astype(jnp.bfloat16)
    query = query * jnp.bfloat16(0.5 * size ** (-0.5))
    lane = lax.broadcasted_iota(jnp.int32, (rows, LANES), 1)
    per_tile = LANES // size
    for tile in range(width // LANES):
        span = slice(tile * LANES, (tile + 1) * LANES)
        whole = query[:, span]
        joined = None
        for head in range(per_tile):
            mine = (lane >= head * size) & (lane < (head + 1) * size)
            part = jnp.where(mine, whole, jnp.zeros_like(whole))
            total = None
            for keys, values, seen in ((keys_a, values_a, first_ref), (keys_b, values_b, second_ref)):
                half = lax.dot_general(
                    part, keys[:, span], (((1,), (1,)), ((), ())), preferred_element_type=jnp.float32
                ).astype(jnp.bfloat16)
                weight = half + half * jnp.tanh(half)
                event = lax.broadcasted_iota(jnp.int32, weight.shape, 1)
                weight = jnp.where(event < seen[...], weight, jnp.zeros_like(weight))
                mixed = jnp.dot(weight, values[:, span], preferred_element_type=jnp.float32)
                total = mixed if total is None else total + mixed
            joined = total if joined is None else jnp.where(mine, total, joined)
        out_ref[:, span] = joined.astype(out_ref.dtype)


def attend(routed, weight, first, second, keys_a, values_a, keys_b, values_b):
    rows, width = routed.shape
    in_vmem = pl.BlockSpec(memory_space=pltpu.VMEM)
    return pl.pallas_call(
        attend_kernel,
        out_shape=jax.ShapeDtypeStruct((rows, width), jnp.bfloat16),
        in_specs=[in_vmem] * 8,
        out_specs=in_vmem,
        compiler_params=pltpu.CompilerParams(vmem_limit_bytes=40 * 2**20),
        name="attend",
    )(routed, weight, first, second, keys_a, values_a, keys_b, values_b)


def per_device(
    item_features,
    tower_in,
    tower_out,
    proj_weight,
    out_weight,
    hist_keys,
    hist_values,
    owner_of,
    row_in,
    hist_lengths,
    causal_offsets,
):
    width = tower_out.shape[1]
    devices = lax.axis_size("seq")
    me = lax.axis_index("seq")
    slot_count, users = row_in.shape
    assert users == 2 and devices % users == 0
    slots = slot_count * users
    rows = item_features.shape[0]
    hist_dev = hist_keys.shape[1]
    depth = max(2, 2 * slots // devices)
    room = devices * depth
    core = me % users
    partner = me + 1 - 2 * core
    swap = [(i, i ^ 1) for i in range(devices)]
    alike = [[b + users * k for k in range(devices // users)] for b in range(users)]

    owners = owner_of.reshape(slots)
    order = jnp.arange(slots, dtype=jnp.int32)
    earlier = (owners[:, None] == owners[None, :]) & (order[None, :] < order[:, None])
    ranks = jnp.sum(earlier.astype(jnp.int32), axis=1)
    code = (owners * depth + ranks) * rows + row_in.reshape(slots)
    codes = lax.all_to_all(
        jnp.broadcast_to(code[None], (devices, slots)), "seq", split_axis=0, concat_axis=0, tiled=True
    )

    def of_user(array, user, axis=0):
        return lax.dynamic_index_in_dim(array, user, axis, keepdims=False)

    keys_b = lax.ppermute(of_user(hist_keys, 1 - core), "seq", swap)
    values_b = lax.ppermute(of_user(hist_values, 1 - core), "seq", swap)
    keys_a = of_user(hist_keys, core)
    values_a = of_user(hist_values, core)

    hidden = jax.nn.silu(
        jnp.dot(item_features, tower_in, preferred_element_type=jnp.float32)
    ).astype(jnp.bfloat16)
    item_embed = jnp.dot(hidden, tower_out, preferred_element_type=jnp.float32).astype(jnp.bfloat16)

    places = codes // rows
    want = me * depth + jnp.arange(depth, dtype=jnp.int32)
    hit = places[:, None, :] == want[None, :, None]
    asked = jnp.sum(jnp.where(hit, (codes % rows)[:, None, :], 0), axis=2).reshape(room)
    picked = jnp.dot(
        (asked[:, None] == jnp.arange(rows, dtype=jnp.int32)[None, :]).astype(jnp.bfloat16),
        item_embed,
        preferred_element_type=jnp.float32,
    ).astype(jnp.bfloat16)
    gathered = lax.all_to_all(
        jnp.broadcast_to(picked[None], (devices // users, room, width)),
        "seq",
        split_axis=0,
        concat_axis=0,
        tiled=True,
        axis_index_groups=alike,
    ).reshape(devices // users * room, width)

    asker = jnp.arange(devices, dtype=jnp.int32)[:, None]
    owner = places // depth
    spot = jnp.where(
        owner % users == core, (owner // users) * room + asker * depth + places % depth, -1
    ).reshape(devices, slot_count, users)
    spot_mine = of_user(spot, core, 2)
    spot_other = of_user(spot, 1 - core, 2)

    def pick(spots):
        chosen = (
            spots[:, None] == jnp.arange(devices // users * room, dtype=jnp.int32)[None, :]
        ).astype(jnp.bfloat16)
        return jnp.dot(chosen, gathered, preferred_element_type=jnp.float32).astype(jnp.bfloat16)

    cands = devices * slot_count
    sent = pick(jnp.concatenate([spot_other.reshape(cands), of_user(spot_mine, partner)]))
    kept = pick(jnp.concatenate([spot_mine.reshape(cands), of_user(spot_other, me)]))
    routed = kept + lax.ppermute(sent, "seq", swap)
    routed_user = routed[:cands]
    own_mine = lax.dynamic_slice_in_dim(routed_user, me * slot_count, slot_count, 0)
    own_other = routed[cands:]
    routed_own = jnp.where(
        core == 0,
        jnp.concatenate([own_mine, own_other]),
        jnp.concatenate([own_other, own_mine]),
    )

    limit = (of_user(hist_lengths, core) - of_user(causal_offsets, core, 1))[:, None]
    user_part = attend(
        routed_user,
        proj_weight[:, 2 * width : 3 * width],
        limit - me * hist_dev,
        limit - partner * hist_dev,
        keys_a,
        values_a,
        keys_b,
        values_b,
    )
    routed_own, user_part = lax.optimization_barrier((routed_own, user_part))
    backs = lax.all_to_all(
        user_part.reshape(devices, slot_count, width), "seq", split_axis=0, concat_axis=0, tiled=True
    )

    proj = jax.nn.silu(jnp.dot(routed_own, proj_weight, preferred_element_type=jnp.float32))
    gate = proj[:, :width]
    value = proj[:, width : 2 * width].astype(jnp.bfloat16)
    query = proj[:, 2 * width : 3 * width].astype(jnp.bfloat16)
    key = proj[:, 3 * width :].astype(jnp.bfloat16)
    own = self_term(query, key, value)

    attended = jnp.sum(
        backs.astype(jnp.float32).reshape(devices // users, slots, width), axis=0
    )
    mixed = (layer_norm(attended + own) * gate).astype(jnp.bfloat16)
    result = routed_own.astype(jnp.float32) + jnp.dot(
        mixed, out_weight, preferred_element_type=jnp.float32
    )
    cand_out = result.astype(jnp.bfloat16).reshape(users, slot_count, width).transpose(1, 0, 2)
    return (item_embed, cand_out)


def solution(mesh):
    return jax.shard_map(
        per_device,
        mesh=mesh,
        in_specs=(
            P(("grp", "seq"), None),
            P(),
            P(),
            P(),
            P(),
            P("grp", "seq", None),
            P("grp", "seq", None),
            P(("grp", "seq"), None, None),
            P(("grp", "seq"), None),
            P("grp"),
            P("grp", None),
        ),
        out_specs=(P(("grp", "seq"), None), P(("grp", "seq"), None, None)),
        check_vma=False,
    )
```

```python
import functools

import jax
import jax.numpy as jnp
from jax import lax
from jax.experimental import pallas as pl
from jax.experimental.pallas import tpu as pltpu
from jax.sharding import PartitionSpec as P

HEADS = 8
LANES = 128


def layer_norm(values):
    centre = values - jnp.mean(values, axis=-1, keepdims=True)
    return centre * lax.rsqrt(jnp.mean(centre * centre, axis=-1, keepdims=True) + 1e-05)


def self_term(query, key, value):
    rows, width = query.shape
    size = width // HEADS
    q_heads = query.astype(jnp.float32).reshape(rows, HEADS, size)
    k_heads = key.astype(jnp.float32).reshape(rows, HEADS, size)
    v_heads = value.astype(jnp.float32).reshape(rows, HEADS, size)
    score = jnp.sum(q_heads * k_heads, axis=-1) * size ** (-0.5)
    return (jax.nn.silu(score)[:, :, None] * v_heads).reshape(rows, width)


def code_kernel(depth, rows, owner_ref, row_ref, out_ref):
    users = owner_ref.shape[0]
    owners = jnp.concatenate([owner_ref[user] for user in range(users)], axis=1)
    wanted = jnp.concatenate([row_ref[user : user + 1, :] for user in range(users)], axis=1)
    slot = lax.broadcasted_iota(jnp.int32, owners.shape, 1)
    ranks = jnp.zeros_like(owners)
    for other in range(owners.shape[1] - 1):
        same = (owners == owners[:, other : other + 1]) & (slot > other)
        ranks = ranks + same.astype(jnp.int32)
    code = (owners * depth + ranks) * rows + wanted
    out_ref[...] = jnp.broadcast_to(code[None], out_ref.shape)


def asked_kernel(depth, codes_ref, embed_ref, out_ref):
    room = codes_ref.shape[0]
    rows = embed_ref.shape[0]
    codes = codes_ref[...]
    rank = lax.rem(lax.broadcasted_iota(jnp.int32, codes.shape, 0), depth)
    hit = lax.div(codes, rows) == lax.axis_index("seq") * depth + rank
    asked = jnp.sum(jnp.where(hit, lax.rem(codes, rows), 0), axis=1, keepdims=True)
    chosen = (lax.broadcasted_iota(jnp.int32, (room, rows), 1) == asked).astype(jnp.bfloat16)
    picked = jnp.dot(chosen, embed_ref[...], preferred_element_type=jnp.float32).astype(jnp.bfloat16)
    for receiver in range(out_ref.shape[0]):
        out_ref[receiver] = picked


def dot_kernel(left_ref, right_ref, out_ref):
    out_ref[...] = jnp.dot(
        left_ref[...], right_ref[...], preferred_element_type=jnp.float32
    ).astype(out_ref.dtype)


def attend_kernel(
    kept_ref, came_ref, weight_ref, seen_ref, keys_a, values_a, keys_b, values_b, out_ref, routed_ref, keys, values, sems
):
    rows, width = out_ref.shape
    size = width // HEADS
    block = keys_b.shape[0]
    core = lax.rem(lax.axis_index("seq"), 2)
    copies = []
    for tile in range(width // LANES):
        span = pl.ds(tile * LANES, LANES)
        for number, (mine, other, target) in enumerate(
            ((keys_a, keys_b, keys), (values_a, values_b, values))
        ):
            here = pl.ds(pl.multiple_of(core * block, block), block)
            there = pl.ds(pl.multiple_of((1 - core) * block, block), block)
            pair = (
                pltpu.make_async_copy(
                    mine.at[core, :, span], target.at[here, span], sems.at[tile, 2 * number]
                ),
                pltpu.make_async_copy(
                    other.at[:, span], target.at[there, span], sems.at[tile, 2 * number + 1]
                ),
            )
            for copy in pair:
                copy.start()
            copies.append(pair)

    routed = kept_ref[...] + came_ref[...]
    routed_ref[...] = routed
    query = jax.nn.silu(
        jnp.dot(routed[:rows], weight_ref[...], preferred_element_type=jnp.float32)
    ).astype(jnp.bfloat16)
    query = query * jnp.bfloat16(0.5 * size ** (-0.5))
    lane = lax.broadcasted_iota(jnp.int32, (rows, LANES), 1)
    per_tile = LANES // size
    for tile in range(width // LANES):
        span = slice(tile * LANES, (tile + 1) * LANES)
        whole = query[:, span]
        joined = None
        for copy in copies[2 * tile]:
            copy.wait()
        for head in range(per_tile):
            mine = (lane >= head * size) & (lane < (head + 1) * size)
            part = jnp.where(mine, whole, jnp.zeros_like(whole))
            half = lax.dot_general(
                part, keys[:, span], (((1,), (1,)), ((), ())), preferred_element_type=jnp.float32
            ).astype(jnp.bfloat16)
            weight = half + half * jnp.tanh(half)
            event = lax.broadcasted_iota(jnp.int32, weight.shape, 1)
            weight = jnp.where(event < seen_ref[...], weight, jnp.zeros_like(weight))
            if head == 0:
                for copy in copies[2 * tile + 1]:
                    copy.wait()
            total = jnp.dot(weight, values[:, span], preferred_element_type=jnp.float32)
            joined = total if joined is None else jnp.where(mine, total, joined)
        out_ref[:, span] = joined.astype(out_ref.dtype)


IN_VMEM = pl.BlockSpec(memory_space=pltpu.VMEM)
ANYWHERE = pl.BlockSpec(memory_space=pl.ANY)


def small_call(kernel, shape, dtype, name, operands):
    return pl.pallas_call(
        kernel,
        out_shape=jax.ShapeDtypeStruct(shape, dtype),
        in_specs=[IN_VMEM] * operands,
        out_specs=IN_VMEM,
        compiler_params=pltpu.CompilerParams(vmem_limit_bytes=24 * 2**20),
        name=name,
    )


def attend(rows, kept, came, weight, seen, keys_a, values_a, keys_b, values_b):
    width = kept.shape[1]
    events = 2 * keys_b.shape[0]
    return pl.pallas_call(
        attend_kernel,
        out_shape=(
            jax.ShapeDtypeStruct((rows, width), jnp.bfloat16),
            jax.ShapeDtypeStruct(kept.shape, jnp.bfloat16),
        ),
        in_specs=[IN_VMEM] * 4 + [ANYWHERE] * 4,
        out_specs=(IN_VMEM, IN_VMEM),
        scratch_shapes=[
            pltpu.VMEM((events, width), jnp.bfloat16),
            pltpu.VMEM((events, width), jnp.bfloat16),
            pltpu.SemaphoreType.DMA((width // LANES, 4)),
        ],
        compiler_params=pltpu.CompilerParams(vmem_limit_bytes=40 * 2**20),
        name="attend",
    )(kept, came, weight, seen, keys_a, values_a, keys_b, values_b)


def per_device(
    item_features,
    tower_in,
    tower_out,
    proj_weight,
    out_weight,
    hist_keys,
    hist_values,
    owner_of,
    row_in,
    hist_lengths,
    causal_offsets,
):
    width = tower_out.shape[1]
    devices = lax.axis_size("seq")
    me = lax.axis_index("seq")
    slot_count, users = row_in.shape
    assert users == 2 and devices % users == 0
    slots = slot_count * users
    rows = item_features.shape[0]
    hist_dev = hist_keys.shape[1]
    depth = max(2, 2 * slots // devices)
    room = devices * depth
    core = me % users
    partner = me + 1 - 2 * core
    swap = [(i, i ^ 1) for i in range(devices)]
    alike = [[b + users * k for k in range(devices // users)] for b in range(users)]

    codes = lax.all_to_all(
        small_call(
            functools.partial(code_kernel, depth, rows), (devices, depth, slots), jnp.int32, "codes", 2
        )(owner_of.transpose(1, 2, 0), row_in.T),
        "seq",
        split_axis=0,
        concat_axis=0,
        tiled=True,
    )

    hidden = jax.nn.silu(
        jnp.dot(item_features, tower_in, preferred_element_type=jnp.float32)
    ).astype(jnp.bfloat16)
    item_embed = jnp.dot(hidden, tower_out, preferred_element_type=jnp.float32).astype(jnp.bfloat16)

    handed = small_call(
        functools.partial(asked_kernel, depth), (devices // users, room, width), jnp.bfloat16, "asked", 2
    )(codes.reshape(room, slots), item_embed)
    gathered = lax.all_to_all(
        handed, "seq", split_axis=0, concat_axis=0, tiled=True, axis_index_groups=alike
    ).reshape(devices // users * room, width)

    def of_user(array, user, axis=0):
        return lax.dynamic_index_in_dim(array, user, axis, keepdims=False)

    handed, give_keys, give_values = lax.optimization_barrier((handed, hist_keys, hist_values))
    keys_b = lax.ppermute(of_user(give_keys, 1 - core), "seq", swap)
    values_b = lax.ppermute(of_user(give_values, 1 - core), "seq", swap)

    places = codes[:, 0] // rows
    asker = jnp.arange(devices, dtype=jnp.int32)[:, None]
    owner = places // depth
    spot = jnp.where(
        owner % users == core, (owner // users) * room + asker * depth + places % depth, -1
    ).reshape(devices, users, slot_count)
    spot_mine = of_user(spot, core, 1)
    spot_other = of_user(spot, 1 - core, 1)

    def choice(spots):
        return (
            spots[:, None] == jnp.arange(devices // users * room, dtype=jnp.int32)[None, :]
        ).astype(jnp.bfloat16)

    cands = devices * slot_count
    choose_sent = choice(jnp.concatenate([spot_other.reshape(cands), of_user(spot_mine, partner)]))
    choose_kept = choice(jnp.concatenate([spot_mine.reshape(cands), of_user(spot_other, me)]))
    choose_sent, choose_kept = lax.optimization_barrier((choose_sent, choose_kept))
    pick = small_call(dot_kernel, (cands + slot_count, width), jnp.bfloat16, "pick", 2)
    sent = pick(choose_sent, gathered)
    kept = pick(choose_kept, gathered)
    came = lax.ppermute(sent, "seq", swap)

    limit = (of_user(hist_lengths, core) - of_user(causal_offsets, core, 1))[:, None]
    user_part, routed = attend(
        cands,
        kept,
        came,
        proj_weight[:, 2 * width : 3 * width],
        limit - (me - core) * hist_dev,
        hist_keys,
        hist_values,
        keys_b,
        values_b,
    )
    backs = lax.all_to_all(
        user_part.reshape(devices, slot_count, width), "seq", split_axis=0, concat_axis=0, tiled=True
    )

    own_mine = lax.dynamic_slice_in_dim(routed, me * slot_count, slot_count, 0)
    own_other = routed[cands:]
    routed_own = jnp.where(
        core == 0,
        jnp.concatenate([own_mine, own_other]),
        jnp.concatenate([own_other, own_mine]),
    )
    proj = jax.nn.silu(jnp.dot(routed_own, proj_weight, preferred_element_type=jnp.float32))
    gate = proj[:, :width]
    value = proj[:, width : 2 * width].astype(jnp.bfloat16)
    query = proj[:, 2 * width : 3 * width].astype(jnp.bfloat16)
    key = proj[:, 3 * width :].astype(jnp.bfloat16)
    own = self_term(query, key, value)

    attended = jnp.sum(
        backs.astype(jnp.float32).reshape(devices // users, slots, width), axis=0
    )
    mixed = (layer_norm(attended + own) * gate).astype(jnp.bfloat16)
    result = routed_own.astype(jnp.float32) + jnp.dot(
        mixed, out_weight, preferred_element_type=jnp.float32
    )
    cand_out = result.astype(jnp.bfloat16).reshape(users, slot_count, width).transpose(1, 0, 2)
    return (item_embed, cand_out)


def solution(mesh):
    return jax.shard_map(
        per_device,
        mesh=mesh,
        in_specs=(
            P(("grp", "seq"), None),
            P(),
            P(),
            P(),
            P(),
            P("grp", "seq", None),
            P("grp", "seq", None),
            P(("grp", "seq"), None, None),
            P(("grp", "seq"), None),
            P("grp"),
            P("grp", None),
        ),
        out_specs=(P(("grp", "seq"), None), P(("grp", "seq"), None, None)),
        check_vma=False,
    )
```

```python
import functools

import jax
import jax.numpy as jnp
from jax import lax
from jax.experimental import pallas as pl
from jax.experimental.pallas import tpu as pltpu
from jax.sharding import PartitionSpec as P

HEADS = 8
LANES = 128


def layer_norm(values):
    centre = values - jnp.mean(values, axis=-1, keepdims=True)
    return centre * lax.rsqrt(jnp.mean(centre * centre, axis=-1, keepdims=True) + 1e-05)


def self_term(query, key, value):
    rows, width = query.shape
    size = width // HEADS
    q_heads = query.astype(jnp.float32).reshape(rows, HEADS, size)
    k_heads = key.astype(jnp.float32).reshape(rows, HEADS, size)
    v_heads = value.astype(jnp.float32).reshape(rows, HEADS, size)
    score = jnp.sum(q_heads * k_heads, axis=-1) * size ** (-0.5)
    return (jax.nn.silu(score)[:, :, None] * v_heads).reshape(rows, width)


def code_kernel(depth, rows, owner_hbm, row_hbm, out_ref, owner_ref, row_ref, sems):
    copies = (
        pltpu.make_async_copy(owner_hbm, owner_ref, sems.at[0]),
        pltpu.make_async_copy(row_hbm, row_ref, sems.at[1]),
    )
    for copy in copies:
        copy.start()
    for copy in copies:
        copy.wait()
    users = owner_ref.shape[0]
    owners = jnp.concatenate([owner_ref[user] for user in range(users)], axis=1)
    wanted = jnp.concatenate([row_ref[user : user + 1, :] for user in range(users)], axis=1)
    slot = lax.broadcasted_iota(jnp.int32, owners.shape, 1)
    ranks = jnp.zeros_like(owners)
    for other in range(owners.shape[1] - 1):
        same = (owners == owners[:, other : other + 1]) & (slot > other)
        ranks = ranks + same.astype(jnp.int32)
    code = (owners * depth + ranks) * rows + wanted
    out_ref[...] = jnp.broadcast_to(code[None], out_ref.shape)


def asked_kernel(depth, codes_ref, embed_ref, out_ref, chosen_ref):
    devices, _, slots = codes_ref.shape
    rows = embed_ref.shape[0]
    want = lax.axis_index("seq") * depth + lax.broadcasted_iota(jnp.int32, (depth, slots), 0)
    lane = lax.broadcasted_iota(jnp.int32, (depth, rows), 1)
    for asker in range(devices):
        codes = jnp.broadcast_to(codes_ref[asker], (depth, slots))
        hit = lax.div(codes, rows) == want
        asked = jnp.sum(jnp.where(hit, lax.rem(codes, rows), 0), axis=1, keepdims=True)
        chosen_ref[asker * depth : (asker + 1) * depth, :] = (lane == asked).astype(jnp.float32)
    picked = jnp.dot(
        chosen_ref[...].astype(jnp.bfloat16), embed_ref[...], preferred_element_type=jnp.float32
    ).astype(jnp.bfloat16)
    for receiver in range(out_ref.shape[0]):
        out_ref[receiver] = picked


def column(row, height):
    down = lax.broadcasted_iota(jnp.int32, (height, row.shape[1]), 0)
    along = lax.broadcasted_iota(jnp.int32, (height, row.shape[1]), 1)
    return jnp.sum(jnp.where(down == along, row, 0), axis=1, keepdims=True)


def ready_kernel(
    depth,
    rows,
    block,
    lengths_ref,
    codes_ref,
    offsets_ref,
    sent_ref,
    kept_ref,
    seen_ref,
):
    devices, _, slots = codes_ref.shape
    users = offsets_ref.shape[0]
    slot_count = slots // users
    room = devices * depth
    me = lax.axis_index("seq")
    core = lax.rem(me, users)
    asker = lax.broadcasted_iota(jnp.int32, codes_ref.shape, 0)
    places = lax.div(codes_ref[...], rows)
    owner = lax.div(places, depth)
    spots = jnp.where(
        lax.rem(owner, users) == core,
        lax.div(owner, users) * room + asker * depth + lax.rem(places, depth),
        -1,
    )
    first = spots[:, :, :slot_count]
    second = spots[:, :, slot_count:]
    mine = jnp.where(core == 0, first, second)
    other = jnp.where(core == 0, second, first)

    def one(array, index):
        return jnp.sum(jnp.where(asker[:, :, :slot_count] == index, array, 0), axis=0)

    cands = devices * slot_count
    blank = jnp.zeros((1, LANES - slot_count), jnp.int32)
    for chosen_ref, all_of, extra in (
        (sent_ref, other, one(mine, me + 1 - 2 * core)),
        (kept_ref, mine, one(other, me)),
    ):
        row = jnp.concatenate([all_of[r] for r in range(devices)] + [extra, blank], axis=1)
        spot = column(row, cands + slot_count)
        place = lax.broadcasted_iota(jnp.int32, chosen_ref.shape, 1)
        chosen_ref[...] = (place == spot).astype(jnp.float32).astype(jnp.bfloat16)

    offsets = jnp.where(core == 0, offsets_ref[0:1, :], offsets_ref[1:2, :])
    seen_ref[...] = column(lengths_ref[core] - (me - core) * block - offsets, cands)


def pick_kernel(chosen_ref, gathered_ref, out_ref):
    out_ref[...] = jnp.dot(
        chosen_ref[...], gathered_ref[...], preferred_element_type=jnp.float32
    ).astype(out_ref.dtype)


def keep_kernel(
    chosen_ref,
    gathered_ref,
    keys_near,
    values_near,
    keys_far,
    values_far,
    proj_hbm,
    out_ref,
    weight_ref,
    keys_ref,
    values_ref,
    sems,
):
    users, block, width = keys_near.shape
    core = lax.rem(lax.axis_index("seq"), users)
    here = pl.ds(pl.multiple_of(core * block, block), block)
    there = pl.ds(pl.multiple_of((1 - core) * block, block), block)
    copies = (
        pltpu.make_async_copy(keys_near.at[core], keys_ref.at[here], sems.at[0]),
        pltpu.make_async_copy(values_near.at[core], values_ref.at[here], sems.at[1]),
        pltpu.make_async_copy(keys_far.at[core], keys_ref.at[there], sems.at[2]),
        pltpu.make_async_copy(values_far.at[core], values_ref.at[there], sems.at[3]),
        pltpu.make_async_copy(proj_hbm.at[:, pl.ds(2 * width, width)], weight_ref, sems.at[4]),
    )
    for copy in copies:
        copy.start()
    pick_kernel(chosen_ref, gathered_ref, out_ref)
    for copy in copies:
        copy.wait()


def attend_kernel(kept_ref, came_ref, weight_ref, seen_ref, keys, values, out_ref, routed_ref):
    rows, width = out_ref.shape
    size = width // HEADS
    routed = kept_ref[...] + came_ref[...]
    routed_ref[...] = routed
    query = jax.nn.silu(
        jnp.dot(routed[:rows], weight_ref[...], preferred_element_type=jnp.float32)
    ).astype(jnp.bfloat16)
    query = query * jnp.bfloat16(0.5 * size ** (-0.5))
    lane = lax.broadcasted_iota(jnp.int32, (rows, LANES), 1)
    per_tile = LANES // size
    for tile in range(width // LANES):
        span = slice(tile * LANES, (tile + 1) * LANES)
        whole = query[:, span]
        joined = None
        for head in range(per_tile):
            mine = (lane >= head * size) & (lane < (head + 1) * size)
            part = jnp.where(mine, whole, jnp.zeros_like(whole))
            half = lax.dot_general(
                part, keys[:, span], (((1,), (1,)), ((), ())), preferred_element_type=jnp.float32
            ).astype(jnp.bfloat16)
            weight = half + half * jnp.tanh(half)
            event = lax.broadcasted_iota(jnp.int32, weight.shape, 1)
            weight = jnp.where(event < seen_ref[...], weight, jnp.zeros_like(weight))
            total = jnp.dot(weight, values[:, span], preferred_element_type=jnp.float32)
            joined = total if joined is None else jnp.where(mine, total, joined)
        out_ref[:, span] = joined.astype(out_ref.dtype)


IN_VMEM = pl.BlockSpec(memory_space=pltpu.VMEM)
IN_SMEM = pl.BlockSpec(memory_space=pltpu.SMEM)
IN_HBM = pl.BlockSpec(memory_space=pltpu.HBM)


def stay(array):
    return pltpu.with_memory_space_constraint(array, pltpu.HBM)


def call(kernel, name, outs, specs, scratch=(), vmem=24):
    many = isinstance(outs, tuple)
    return pl.pallas_call(
        kernel,
        out_shape=outs,
        in_specs=specs,
        out_specs=(IN_VMEM,) * len(outs) if many else IN_VMEM,
        scratch_shapes=scratch,
        compiler_params=pltpu.CompilerParams(vmem_limit_bytes=vmem * 2**20),
        name=name,
    )


def shaped(shape, dtype=jnp.bfloat16):
    return jax.ShapeDtypeStruct(shape, dtype)


def per_device(
    item_features,
    tower_in,
    tower_out,
    proj_weight,
    out_weight,
    hist_keys,
    hist_values,
    owner_of,
    row_in,
    hist_lengths,
    causal_offsets,
):
    width = tower_out.shape[1]
    devices = lax.axis_size("seq")
    me = lax.axis_index("seq")
    slot_count, users = row_in.shape
    assert users == 2 and devices % users == 0
    slots = slot_count * users
    rows = item_features.shape[0]
    hist_dev = hist_keys.shape[1]
    depth = max(2, 2 * slots // devices)
    room = devices * depth
    core = me % users
    swap = [(i, i ^ 1) for i in range(devices)]
    alike = [[b + users * k for k in range(devices // users)] for b in range(users)]

    half = devices // users
    cands = devices * slot_count

    codes = lax.all_to_all(
        call(
            functools.partial(code_kernel, depth, rows),
            "codes",
            shaped((devices, 1, slots), jnp.int32),
            [IN_HBM] * 2,
            [
                pltpu.VMEM((users, 1, slot_count), jnp.int32),
                pltpu.VMEM((users, slot_count), jnp.int32),
                pltpu.SemaphoreType.DMA((2,)),
            ],
        )(stay(owner_of.transpose(1, 2, 0)), stay(row_in.T)),
        "seq",
        split_axis=0,
        concat_axis=0,
        tiled=True,
    )

    keys_far = lax.ppermute(hist_keys, "seq", swap)
    values_far = lax.ppermute(hist_values, "seq", swap)

    hidden = jax.nn.silu(
        jnp.dot(item_features, tower_in, preferred_element_type=jnp.float32)
    ).astype(jnp.bfloat16)
    item_embed = jnp.dot(hidden, tower_out, preferred_element_type=jnp.float32).astype(jnp.bfloat16)

    handed = call(
        functools.partial(asked_kernel, depth),
        "asked",
        shaped((half, room, width)),
        [IN_VMEM] * 2,
        [pltpu.VMEM((room, rows), jnp.float32)],
    )(codes, item_embed)
    gathered = lax.all_to_all(
        handed, "seq", split_axis=0, concat_axis=0, tiled=True, axis_index_groups=alike
    ).reshape(half * room, width)

    chosen = shaped((cands + slot_count, half * room))
    events = users * hist_dev
    choose_sent, choose_kept, seen = call(
        functools.partial(ready_kernel, depth, rows, hist_dev),
        "ready",
        (chosen, chosen, shaped((cands, 1), jnp.int32)),
        [IN_SMEM] + [IN_VMEM] * 2,
    )(hist_lengths, codes, causal_offsets.T)

    taken = shaped((cands + slot_count, width))
    sent = call(pick_kernel, "pick", taken, [IN_VMEM] * 2)(choose_sent, gathered)
    came = lax.ppermute(sent, "seq", swap)
    kept, weight, keys, values = call(
        keep_kernel,
        "keep",
        (taken, shaped((width, width)), shaped((events, width)), shaped((events, width))),
        [IN_VMEM] * 2 + [IN_HBM] * 5,
        [pltpu.SemaphoreType.DMA((5,))],
    )(
        choose_kept,
        gathered,
        stay(hist_keys),
        stay(hist_values),
        stay(keys_far),
        stay(values_far),
        stay(proj_weight),
    )

    user_part, routed = call(
        attend_kernel,
        "attend",
        (shaped((cands, width)), shaped((cands + slot_count, width))),
        [IN_VMEM] * 6,
        vmem=48,
    )(kept, came, weight, seen, keys, values)
    backs = lax.all_to_all(
        user_part.reshape(devices, slot_count, width), "seq", split_axis=0, concat_axis=0, tiled=True
    )

    own_mine = lax.dynamic_slice_in_dim(routed, me * slot_count, slot_count, 0)
    own_other = routed[cands:]
    routed_own = jnp.where(
        core == 0,
        jnp.concatenate([own_mine, own_other]),
        jnp.concatenate([own_other, own_mine]),
    )
    proj = jax.nn.silu(jnp.dot(routed_own, proj_weight, preferred_element_type=jnp.float32))
    gate = proj[:, :width]
    value = proj[:, width : 2 * width].astype(jnp.bfloat16)
    query = proj[:, 2 * width : 3 * width].astype(jnp.bfloat16)
    key = proj[:, 3 * width :].astype(jnp.bfloat16)
    own = self_term(query, key, value)

    attended = jnp.sum(
        backs.astype(jnp.float32).reshape(devices // users, slots, width), axis=0
    )
    mixed = (layer_norm(attended + own) * gate).astype(jnp.bfloat16)
    result = routed_own.astype(jnp.float32) + jnp.dot(
        mixed, out_weight, preferred_element_type=jnp.float32
    )
    cand_out = result.astype(jnp.bfloat16).reshape(users, slot_count, width).transpose(1, 0, 2)
    return (item_embed, cand_out)


def solution(mesh):
    return jax.shard_map(
        per_device,
        mesh=mesh,
        in_specs=(
            P(("grp", "seq"), None),
            P(),
            P(),
            P(),
            P(),
            P("grp", "seq", None),
            P("grp", "seq", None),
            P(("grp", "seq"), None, None),
            P(("grp", "seq"), None),
            P("grp"),
            P("grp", None),
        ),
        out_specs=(P(("grp", "seq"), None), P(("grp", "seq"), None, None)),
        check_vma=False,
    )
```

```python
import functools

import jax
import jax.numpy as jnp
from jax import lax
from jax.experimental import pallas as pl
from jax.experimental.pallas import tpu as pltpu
from jax.sharding import PartitionSpec as P


HEADS = 8
LANES = 128


def layer_norm(values):
    centre = values - jnp.mean(values, axis=-1, keepdims=True)
    return centre * lax.rsqrt(jnp.mean(centre * centre, axis=-1, keepdims=True) + 1e-05)


def self_term(query, key, value):
    rows, width = query.shape
    size = width // HEADS
    q_heads = query.astype(jnp.float32).reshape(rows, HEADS, size)
    k_heads = key.astype(jnp.float32).reshape(rows, HEADS, size)
    v_heads = value.astype(jnp.float32).reshape(rows, HEADS, size)
    score = jnp.sum(q_heads * k_heads, axis=-1) * size ** (-0.5)
    return (jax.nn.silu(score)[:, :, None] * v_heads).reshape(rows, width)


def ring_order(chips):
    ring = list(range(0, chips, 2)) + list(range(1, chips, 2))[::-1]
    start = ring.index(min(chips - 1, (chips // 2) | 1))
    return ring[start:] + ring[:start]


def middle_order(chips):
    return sorted(range(chips), key=lambda chip: abs(2 * (chip - chips // 2) + 0.5))


def place_in(order, chip):
    place = jnp.zeros_like(chip)
    for number, other in enumerate(order):
        place = jnp.where(chip == other, number, place)
    return place


def code_kernel(depth, rows, owner_hbm, row_hbm, out_ref, owner_ref, row_ref, sems):
    copies = (
        pltpu.make_async_copy(owner_hbm, owner_ref, sems.at[0]),
        pltpu.make_async_copy(row_hbm, row_ref, sems.at[1]),
    )
    for copy in copies:
        copy.start()
    for copy in copies:
        copy.wait()
    users = owner_ref.shape[0]
    owners = jnp.concatenate([owner_ref[user] for user in range(users)], axis=1)
    wanted = jnp.concatenate([row_ref[user : user + 1, :] for user in range(users)], axis=1)
    slot = lax.broadcasted_iota(jnp.int32, owners.shape, 1)
    ranks = jnp.zeros_like(owners)
    for other in range(owners.shape[1] - 1):
        same = (owners == owners[:, other : other + 1]) & (slot > other)
        ranks = ranks + same.astype(jnp.int32)
    code = (owners * depth + ranks) * rows + wanted
    out_ref[...] = jnp.broadcast_to(code[None], out_ref.shape)


def asked_kernel(depth, codes_ref, embed_ref, out_hbm, chosen_ref, picked_ref, sems):
    devices, _, slots = codes_ref.shape
    rows = embed_ref.shape[0]
    want = lax.axis_index("seq") * depth + lax.broadcasted_iota(jnp.int32, (depth, slots), 0)
    lane = lax.broadcasted_iota(jnp.int32, (depth, rows), 1)
    for asker in range(devices):
        codes = jnp.broadcast_to(codes_ref[asker], (depth, slots))
        hit = lax.div(codes, rows) == want
        asked = jnp.sum(jnp.where(hit, lax.rem(codes, rows), 0), axis=1, keepdims=True)
        chosen_ref[asker * depth : (asker + 1) * depth, :] = (lane == asked).astype(jnp.float32)
    picked_ref[...] = jnp.dot(
        chosen_ref[...].astype(jnp.bfloat16), embed_ref[...], preferred_element_type=jnp.float32
    ).astype(jnp.bfloat16)
    copies = [
        pltpu.make_async_copy(picked_ref, out_hbm.at[receiver], sems.at[receiver])
        for receiver in range(out_hbm.shape[0])
    ]
    for copy in copies:
        copy.start()
    for copy in copies:
        copy.wait()


def column(row, height):
    down = lax.broadcasted_iota(jnp.int32, (height, row.shape[1]), 0)
    along = lax.broadcasted_iota(jnp.int32, (height, row.shape[1]), 1)
    return jnp.sum(jnp.where(down == along, row, 0), axis=1, keepdims=True)


def ready_kernel(
    depth,
    rows,
    block,
    order,
    handing,
    lengths_ref,
    codes_ref,
    offsets_ref,
    sent_ref,
    kept_ref,
    seen_ref,
):
    devices, _, slots = codes_ref.shape
    users = offsets_ref.shape[0]
    slot_count = slots // users
    room = devices * depth
    me = lax.axis_index("seq")
    core = lax.rem(me, users)
    mine_at = place_in(order, lax.div(me, users)) * users + core
    asker = lax.broadcasted_iota(jnp.int32, codes_ref.shape, 0)
    places = lax.div(codes_ref[...], rows)
    owner = lax.div(places, depth)
    spots = jnp.where(
        lax.rem(owner, users) == core,
        place_in(handing, lax.div(owner, users)) * room + asker * depth + lax.rem(places, depth),
        -1,
    )
    first = spots[:, :, :slot_count]
    second = spots[:, :, slot_count:]
    mine = jnp.where(core == 0, first, second)
    other = jnp.where(core == 0, second, first)

    def one(array, index):
        return jnp.sum(jnp.where(asker[:, :, :slot_count] == index, array, 0), axis=0)

    cands = devices * slot_count
    blank = jnp.zeros((1, LANES - slot_count), jnp.int32)
    for chosen_ref, all_of, extra in (
        (sent_ref, other, one(mine, mine_at + 1 - 2 * core)),
        (kept_ref, mine, one(other, mine_at)),
    ):
        row = jnp.concatenate([all_of[r] for r in range(devices)] + [extra, blank], axis=1)
        spot = column(row, cands + slot_count)
        place = lax.broadcasted_iota(jnp.int32, chosen_ref.shape, 1)
        chosen_ref[...] = (place == spot).astype(jnp.float32).astype(jnp.bfloat16)

    offsets = jnp.where(core == 0, offsets_ref[0:1, :], offsets_ref[1:2, :])
    offsets = jnp.concatenate(
        [
            offsets[:, slot_count * device : slot_count * (device + 1)]
            for device in (users * chip + other for chip in order for other in range(users))
        ],
        axis=1,
    )
    seen_ref[...] = column(lengths_ref[core] - (me - core) * block - offsets, cands)


def pick_kernel(chosen_ref, gathered_ref, out_ref):
    out_ref[...] = jnp.dot(
        chosen_ref[...], gathered_ref[...], preferred_element_type=jnp.float32
    ).astype(out_ref.dtype)


def keep_kernel(
    chosen_ref,
    gathered_ref,
    keys_near,
    values_near,
    keys_far,
    values_far,
    proj_hbm,
    out_ref,
    weight_ref,
    keys_ref,
    values_ref,
    sems,
):
    users, block, width = keys_near.shape
    core = lax.rem(lax.axis_index("seq"), users)
    here = pl.ds(pl.multiple_of(core * block, block), block)
    there = pl.ds(pl.multiple_of((1 - core) * block, block), block)
    copies = (
        pltpu.make_async_copy(keys_near.at[core], keys_ref.at[here], sems.at[0]),
        pltpu.make_async_copy(values_near.at[core], values_ref.at[here], sems.at[1]),
        pltpu.make_async_copy(keys_far.at[core], keys_ref.at[there], sems.at[2]),
        pltpu.make_async_copy(values_far.at[core], values_ref.at[there], sems.at[3]),
        pltpu.make_async_copy(proj_hbm.at[:, pl.ds(2 * width, width)], weight_ref, sems.at[4]),
    )
    for copy in copies:
        copy.start()
    pick_kernel(chosen_ref, gathered_ref, out_ref)
    for copy in copies:
        copy.wait()


def attend_kernel(kept_ref, came_ref, weight_ref, seen_ref, keys, values, out_ref, routed_ref):
    rows, width = out_ref.shape
    size = width // HEADS
    routed = kept_ref[...] + came_ref[...]
    routed_ref[...] = routed
    query = jax.nn.silu(
        jnp.dot(routed[:rows], weight_ref[...], preferred_element_type=jnp.float32)
    ).astype(jnp.bfloat16)
    query = query * jnp.bfloat16(0.5 * size ** (-0.5))
    event = lax.broadcasted_iota(jnp.int32, (rows, keys.shape[0]), 1)
    shown = (event < seen_ref[...]).astype(jnp.float32).astype(jnp.bfloat16)
    lane = lax.broadcasted_iota(jnp.int32, (rows, LANES), 1)
    per_tile = LANES // size
    for tile in range(width // LANES):
        span = slice(tile * LANES, (tile + 1) * LANES)
        whole = query[:, span]
        joined = None
        for head in range(per_tile):
            mine = (lane >= head * size) & (lane < (head + 1) * size)
            part = jnp.where(mine, whole, jnp.zeros_like(whole))
            half = lax.dot_general(
                part, keys[:, span], (((1,), (1,)), ((), ())), preferred_element_type=jnp.float32
            ).astype(jnp.bfloat16)
            weight = half + half * jnp.tanh(half)
            weight = weight * shown
            total = jnp.dot(weight, values[:, span], preferred_element_type=jnp.float32)
            joined = total if joined is None else jnp.where(mine, total, joined)
        out_ref[:, span] = joined.astype(out_ref.dtype)


IN_VMEM = pl.BlockSpec(memory_space=pltpu.VMEM)
IN_SMEM = pl.BlockSpec(memory_space=pltpu.SMEM)
IN_HBM = pl.BlockSpec(memory_space=pltpu.HBM)


def stay(array):
    return pltpu.with_memory_space_constraint(array, pltpu.HBM)


def call(kernel, outs, specs, scratch=(), vmem=24, out_space=IN_VMEM):
    many = isinstance(outs, tuple)
    return pl.pallas_call(
        kernel,
        out_shape=outs,
        in_specs=specs,
        out_specs=(out_space,) * len(outs) if many else out_space,
        scratch_shapes=scratch,
        compiler_params=pltpu.CompilerParams(vmem_limit_bytes=vmem * 2**20),
    )


def shaped(shape, dtype=jnp.bfloat16):
    return jax.ShapeDtypeStruct(shape, dtype)


def per_device(
    item_features,
    tower_in,
    tower_out,
    proj_weight,
    out_weight,
    hist_keys,
    hist_values,
    owner_of,
    row_in,
    hist_lengths,
    causal_offsets,
):
    width = tower_out.shape[1]
    devices = lax.axis_size("seq")
    me = lax.axis_index("seq")
    slot_count, users = row_in.shape
    assert users == 2 and devices % users == 0
    slots = slot_count * users
    rows = item_features.shape[0]
    hist_dev = hist_keys.shape[1]
    depth = max(2, 2 * slots // devices)
    room = devices * depth
    core = me % users
    swap = [(i, i ^ 1) for i in range(devices)]
    half = devices // users
    order = ring_order(half)
    handing = middle_order(half)
    everyone = [[users * chip + other for chip in order for other in range(users)]]
    alike = [[users * chip + other for chip in handing] for other in range(users)]
    mine_at = place_in(order, me // users) * users + core
    cands = devices * slot_count

    codes = lax.all_to_all(
        call(
            functools.partial(code_kernel, depth, rows),
            shaped((devices, 1, slots), jnp.int32),
            [IN_HBM] * 2,
            [
                pltpu.VMEM((users, 1, slot_count), jnp.int32),
                pltpu.VMEM((users, slot_count), jnp.int32),
                pltpu.SemaphoreType.DMA((2,)),
            ],
        )(stay(owner_of.transpose(1, 2, 0)), stay(row_in.T)),
        "seq",
        split_axis=0,
        concat_axis=0,
        tiled=True,
        axis_index_groups=everyone,
    )

    keys_far = lax.ppermute(hist_keys, "seq", swap)
    values_far = lax.ppermute(hist_values, "seq", swap)

    hidden = jax.nn.silu(
        jnp.dot(item_features, tower_in, preferred_element_type=jnp.float32)
    ).astype(jnp.bfloat16)
    item_embed = jnp.dot(hidden, tower_out, preferred_element_type=jnp.float32).astype(jnp.bfloat16)

    handed = call(
        functools.partial(asked_kernel, depth),
        shaped((half, room, width)),
        [IN_VMEM] * 2,
        [
            pltpu.VMEM((room, rows), jnp.float32),
            pltpu.VMEM((room, width), jnp.bfloat16),
            pltpu.SemaphoreType.DMA((half,)),
        ],
        out_space=IN_HBM,
    )(codes, item_embed)
    gathered = lax.all_to_all(
        handed, "seq", split_axis=0, concat_axis=0, tiled=True, axis_index_groups=alike
    )
    gathered = gathered.reshape(half * room, width)

    chosen = shaped((cands + slot_count, half * room))
    events = users * hist_dev
    choose_sent, choose_kept, seen = call(
        functools.partial(ready_kernel, depth, rows, hist_dev, order, handing),
        (chosen, chosen, shaped((cands, 1), jnp.int32)),
        [IN_SMEM] + [IN_VMEM] * 2,
    )(hist_lengths, codes, causal_offsets.T)

    taken = shaped((cands + slot_count, width))
    sent = call(pick_kernel, taken, [IN_VMEM] * 2)(choose_sent, gathered)
    came = lax.ppermute(sent, "seq", swap)
    kept, weight, keys, values = call(
        keep_kernel,
        (taken, shaped((width, width)), shaped((events, width)), shaped((events, width))),
        [IN_VMEM] * 2 + [IN_HBM] * 5,
        [pltpu.SemaphoreType.DMA((5,))],
    )(
        choose_kept,
        gathered,
        stay(hist_keys),
        stay(hist_values),
        stay(keys_far),
        stay(values_far),
        stay(proj_weight),
    )

    user_part, routed = call(
        attend_kernel,
        (shaped((cands, width)), shaped((cands + slot_count, width))),
        [IN_VMEM] * 6,
        vmem=48,
    )(kept, came, weight, seen, keys, values)
    backs = lax.all_to_all(
        user_part.reshape(devices, slot_count, width),
        "seq",
        split_axis=0,
        concat_axis=0,
        tiled=True,
        axis_index_groups=everyone,
    )

    own_mine = lax.dynamic_slice_in_dim(routed, mine_at * slot_count, slot_count, 0)
    own_other = routed[cands:]
    routed_own = jnp.where(
        core == 0,
        jnp.concatenate([own_mine, own_other]),
        jnp.concatenate([own_other, own_mine]),
    )
    proj = jax.nn.silu(jnp.dot(routed_own, proj_weight, preferred_element_type=jnp.float32))
    gate = proj[:, :width]
    value = proj[:, width : 2 * width].astype(jnp.bfloat16)
    query = proj[:, 2 * width : 3 * width].astype(jnp.bfloat16)
    key = proj[:, 3 * width :].astype(jnp.bfloat16)
    own = self_term(query, key, value)

    attended = jnp.sum(
        backs.astype(jnp.float32).reshape(devices // users, slots, width), axis=0
    )
    mixed = (layer_norm(attended + own) * gate).astype(jnp.bfloat16)
    result = routed_own.astype(jnp.float32) + jnp.dot(
        mixed, out_weight, preferred_element_type=jnp.float32
    )
    cand_out = result.astype(jnp.bfloat16).reshape(users, slot_count, width).transpose(1, 0, 2)
    return (item_embed, cand_out)


def solution(mesh):
    return jax.shard_map(
        per_device,
        mesh=mesh,
        in_specs=(
            P(("grp", "seq"), None),
            P(),
            P(),
            P(),
            P(),
            P("grp", "seq", None),
            P("grp", "seq", None),
            P(("grp", "seq"), None, None),
            P(("grp", "seq"), None),
            P("grp"),
            P("grp", None),
        ),
        out_specs=(P(("grp", "seq"), None), P(("grp", "seq"), None, None)),
        check_vma=False,
    )
```

```python
import functools

import jax
import jax.numpy as jnp
from jax import lax
from jax.experimental import pallas as pl
from jax.experimental.pallas import tpu as pltpu
from jax.sharding import PartitionSpec as P


HEADS = 8
LANES = 128


def layer_norm(values):
    centre = values - jnp.mean(values, axis=-1, keepdims=True)
    return centre * lax.rsqrt(jnp.mean(centre * centre, axis=-1, keepdims=True) + 1e-05)


def self_term(query, key, value):
    rows, width = query.shape
    size = width // HEADS
    q_heads = query.astype(jnp.float32).reshape(rows, HEADS, size)
    k_heads = key.astype(jnp.float32).reshape(rows, HEADS, size)
    v_heads = value.astype(jnp.float32).reshape(rows, HEADS, size)
    score = jnp.sum(q_heads * k_heads, axis=-1) * size ** (-0.5)
    return (jax.nn.silu(score)[:, :, None] * v_heads).reshape(rows, width)


def ring_order(chips):
    ring = list(range(1, chips, 2)) + list(range(0, chips, 2))[::-1]
    start = ring.index(min(chips - 1, (chips // 2) | 1))
    return ring[start:] + ring[:start]


def middle_order(chips):
    return [(chips // 2 + step) % chips for step in range(chips)]


def place_in(order, chip):
    place = jnp.zeros_like(chip)
    for number, other in enumerate(order):
        place = jnp.where(chip == other, number, place)
    return place


def code_kernel(depth, rows, owner_hbm, row_hbm, out_ref, owner_ref, row_ref, sems):
    copies = (
        pltpu.make_async_copy(owner_hbm, owner_ref, sems.at[0]),
        pltpu.make_async_copy(row_hbm, row_ref, sems.at[1]),
    )
    for copy in copies:
        copy.start()
    for copy in copies:
        copy.wait()
    users = owner_ref.shape[0]
    owners = jnp.concatenate([owner_ref[user] for user in range(users)], axis=1)
    wanted = jnp.concatenate([row_ref[user : user + 1, :] for user in range(users)], axis=1)
    slot = lax.broadcasted_iota(jnp.int32, owners.shape, 1)
    ranks = jnp.zeros_like(owners)
    for other in range(owners.shape[1] - 1):
        same = (owners == owners[:, other : other + 1]) & (slot > other)
        ranks = ranks + same.astype(jnp.int32)
    code = (owners * depth + ranks) * rows + wanted
    out_ref[...] = jnp.broadcast_to(code[None], out_ref.shape)


def asked_kernel(depth, codes_ref, embed_ref, out_hbm, chosen_ref, picked_ref, sems):
    devices, _, slots = codes_ref.shape
    rows = embed_ref.shape[0]
    want = lax.axis_index("seq") * depth + lax.broadcasted_iota(jnp.int32, (depth, slots), 0)
    lane = lax.broadcasted_iota(jnp.int32, (depth, rows), 1)
    for asker in range(devices):
        codes = jnp.broadcast_to(codes_ref[asker], (depth, slots))
        hit = lax.div(codes, rows) == want
        asked = jnp.sum(jnp.where(hit, lax.rem(codes, rows), 0), axis=1, keepdims=True)
        chosen_ref[asker * depth : (asker + 1) * depth, :] = (lane == asked).astype(jnp.float32)
    picked_ref[...] = jnp.dot(
        chosen_ref[...].astype(jnp.bfloat16), embed_ref[...], preferred_element_type=jnp.float32
    ).astype(jnp.bfloat16)
    copies = [
        pltpu.make_async_copy(picked_ref, out_hbm.at[receiver], sems.at[receiver])
        for receiver in range(out_hbm.shape[0])
    ]
    for copy in copies:
        copy.start()
    for copy in copies:
        copy.wait()


def column(row, height):
    down = lax.broadcasted_iota(jnp.int32, (height, row.shape[1]), 0)
    along = lax.broadcasted_iota(jnp.int32, (height, row.shape[1]), 1)
    return jnp.sum(jnp.where(down == along, row, 0), axis=1, keepdims=True)


def ready_kernel(
    depth,
    rows,
    block,
    order,
    handing,
    lengths_ref,
    codes_ref,
    offsets_ref,
    sent_ref,
    kept_ref,
    seen_ref,
):
    devices, _, slots = codes_ref.shape
    users = offsets_ref.shape[0]
    slot_count = slots // users
    room = devices * depth
    me = lax.axis_index("seq")
    core = lax.rem(me, users)
    mine_at = place_in(order, lax.div(me, users)) * users + core
    asker = lax.broadcasted_iota(jnp.int32, codes_ref.shape, 0)
    places = lax.div(codes_ref[...], rows)
    owner = lax.div(places, depth)
    spots = jnp.where(
        lax.rem(owner, users) == core,
        place_in(handing, lax.div(owner, users)) * room + asker * depth + lax.rem(places, depth),
        -1,
    )
    first = spots[:, :, :slot_count]
    second = spots[:, :, slot_count:]
    mine = jnp.where(core == 0, first, second)
    other = jnp.where(core == 0, second, first)

    def one(array, index):
        return jnp.sum(jnp.where(asker[:, :, :slot_count] == index, array, 0), axis=0)

    cands = devices * slot_count
    blank = jnp.zeros((1, LANES - slot_count), jnp.int32)
    for chosen_ref, all_of, extra in (
        (sent_ref, other, one(mine, mine_at + 1 - 2 * core)),
        (kept_ref, mine, one(other, mine_at)),
    ):
        row = jnp.concatenate([all_of[r] for r in range(devices)] + [extra, blank], axis=1)
        spot = column(row, cands + slot_count)
        place = lax.broadcasted_iota(jnp.int32, chosen_ref.shape, 1)
        chosen_ref[...] = (place == spot).astype(jnp.float32).astype(jnp.bfloat16)

    offsets = jnp.where(core == 0, offsets_ref[0:1, :], offsets_ref[1:2, :])
    offsets = jnp.concatenate(
        [
            offsets[:, slot_count * device : slot_count * (device + 1)]
            for device in (users * chip + other for chip in order for other in range(users))
        ],
        axis=1,
    )
    seen_ref[...] = column(lengths_ref[core] - (me - core) * block - offsets, cands)


def pick_kernel(chosen_ref, gathered_ref, out_ref):
    out_ref[...] = jnp.dot(
        chosen_ref[...], gathered_ref[...], preferred_element_type=jnp.float32
    ).astype(out_ref.dtype)


def keep_kernel(
    chosen_ref,
    gathered_ref,
    keys_near,
    values_near,
    keys_far,
    values_far,
    proj_hbm,
    out_ref,
    weight_ref,
    keys_ref,
    values_ref,
    sems,
):
    users, block, width = keys_near.shape
    core = lax.rem(lax.axis_index("seq"), users)
    here = pl.ds(pl.multiple_of(core * block, block), block)
    there = pl.ds(pl.multiple_of((1 - core) * block, block), block)
    copies = (
        pltpu.make_async_copy(keys_near.at[core], keys_ref.at[here], sems.at[0]),
        pltpu.make_async_copy(values_near.at[core], values_ref.at[here], sems.at[1]),
        pltpu.make_async_copy(keys_far.at[core], keys_ref.at[there], sems.at[2]),
        pltpu.make_async_copy(values_far.at[core], values_ref.at[there], sems.at[3]),
        pltpu.make_async_copy(proj_hbm.at[:, pl.ds(2 * width, width)], weight_ref, sems.at[4]),
    )
    for copy in copies:
        copy.start()
    pick_kernel(chosen_ref, gathered_ref, out_ref)
    for copy in copies:
        copy.wait()


def attend_kernel(kept_ref, came_ref, weight_ref, seen_ref, keys, values, out_ref, routed_ref):
    rows, width = out_ref.shape
    size = width // HEADS
    routed = kept_ref[...] + came_ref[...]
    routed_ref[...] = routed
    query = jax.nn.silu(
        jnp.dot(routed[:rows], weight_ref[...], preferred_element_type=jnp.float32)
    ).astype(jnp.bfloat16)
    query = query * jnp.bfloat16(0.5 * size ** (-0.5))
    event = lax.broadcasted_iota(jnp.int32, (rows, keys.shape[0]), 1)
    shown = (event < seen_ref[...]).astype(jnp.float32).astype(jnp.bfloat16)
    lane = lax.broadcasted_iota(jnp.int32, (rows, LANES), 1)
    per_tile = LANES // size
    for tile in range(width // LANES):
        span = slice(tile * LANES, (tile + 1) * LANES)
        whole = query[:, span]
        joined = None
        for head in range(per_tile):
            mine = (lane >= head * size) & (lane < (head + 1) * size)
            part = jnp.where(mine, whole, jnp.zeros_like(whole))
            half = lax.dot_general(
                part, keys[:, span], (((1,), (1,)), ((), ())), preferred_element_type=jnp.float32
            ).astype(jnp.bfloat16)
            weight = half + half * jnp.tanh(half)
            weight = weight * shown
            total = jnp.dot(weight, values[:, span], preferred_element_type=jnp.float32)
            joined = total if joined is None else jnp.where(mine, total, joined)
        out_ref[:, span] = joined.astype(out_ref.dtype)


def finish_kernel(backs_ref, own_ref, gate_ref, routed_ref, weight_ref, out_ref):
    slot_count, users, _ = out_ref.shape
    chips = backs_ref.shape[0] // users
    attended = []
    for user in range(users):
        parts = [backs_ref[chip * users + user].astype(jnp.float32) for chip in range(chips)]
        while len(parts) > 1:
            parts = [sum(parts[k : k + 2][1:], parts[k]) for k in range(0, len(parts), 2)]
        attended.append(parts[0])
    total = jnp.concatenate(attended, axis=0) + own_ref[...]
    mixed = (layer_norm(total) * gate_ref[...]).astype(jnp.bfloat16)
    result = routed_ref[...].astype(jnp.float32) + jnp.dot(
        mixed, weight_ref[...], preferred_element_type=jnp.float32
    )
    for cand in range(slot_count):
        rows = [result[user * slot_count + cand : user * slot_count + cand + 1] for user in range(users)]
        out_ref[cand] = jnp.concatenate(rows, axis=0).astype(out_ref.dtype)


IN_VMEM = pl.BlockSpec(memory_space=pltpu.VMEM)
IN_SMEM = pl.BlockSpec(memory_space=pltpu.SMEM)
IN_HBM = pl.BlockSpec(memory_space=pltpu.HBM)


def stay(array):
    return pltpu.with_memory_space_constraint(array, pltpu.HBM)


def call(kernel, outs, specs, scratch=(), vmem=24, out_space=IN_VMEM):
    many = isinstance(outs, tuple)
    return pl.pallas_call(
        kernel,
        out_shape=outs,
        in_specs=specs,
        out_specs=(out_space,) * len(outs) if many else out_space,
        scratch_shapes=scratch,
        compiler_params=pltpu.CompilerParams(vmem_limit_bytes=vmem * 2**20),
    )


def shaped(shape, dtype=jnp.bfloat16):
    return jax.ShapeDtypeStruct(shape, dtype)


def per_device(
    item_features,
    tower_in,
    tower_out,
    proj_weight,
    out_weight,
    hist_keys,
    hist_values,
    owner_of,
    row_in,
    hist_lengths,
    causal_offsets,
):
    width = tower_out.shape[1]
    devices = lax.axis_size("seq")
    me = lax.axis_index("seq")
    slot_count, users = row_in.shape
    assert users == 2 and devices % users == 0
    slots = slot_count * users
    rows = item_features.shape[0]
    hist_dev = hist_keys.shape[1]
    depth = max(2, 2 * slots // devices)
    room = devices * depth
    core = me % users
    swap = [(i, i ^ 1) for i in range(devices)]
    half = devices // users
    order = ring_order(half)
    handing = middle_order(half)
    everyone = [[users * chip + other for chip in order for other in range(users)]]
    alike = [[users * chip + other for chip in handing] for other in range(users)]
    mine_at = place_in(order, me // users) * users + core
    cands = devices * slot_count

    codes = lax.all_to_all(
        call(
            functools.partial(code_kernel, depth, rows),
            shaped((devices, 1, slots), jnp.int32),
            [IN_HBM] * 2,
            [
                pltpu.VMEM((users, 1, slot_count), jnp.int32),
                pltpu.VMEM((users, slot_count), jnp.int32),
                pltpu.SemaphoreType.DMA((2,)),
            ],
        )(stay(owner_of.transpose(1, 2, 0)), stay(row_in.T)),
        "seq",
        split_axis=0,
        concat_axis=0,
        tiled=True,
        axis_index_groups=everyone,
    )

    keys_far = lax.ppermute(hist_keys, "seq", swap)
    values_far = lax.ppermute(hist_values, "seq", swap)

    hidden = jax.nn.silu(
        jnp.dot(item_features, tower_in, preferred_element_type=jnp.float32)
    ).astype(jnp.bfloat16)
    item_embed = jnp.dot(hidden, tower_out, preferred_element_type=jnp.float32).astype(jnp.bfloat16)

    handed = call(
        functools.partial(asked_kernel, depth),
        shaped((half, room, width)),
        [IN_VMEM] * 2,
        [
            pltpu.VMEM((room, rows), jnp.float32),
            pltpu.VMEM((room, width), jnp.bfloat16),
            pltpu.SemaphoreType.DMA((half,)),
        ],
        out_space=IN_HBM,
    )(codes, item_embed)
    gathered = lax.all_to_all(
        handed, "seq", split_axis=0, concat_axis=0, tiled=True, axis_index_groups=alike
    )
    gathered = gathered.reshape(half * room, width)

    chosen = shaped((cands + slot_count, half * room))
    events = users * hist_dev
    choose_sent, choose_kept, seen = call(
        functools.partial(ready_kernel, depth, rows, hist_dev, order, handing),
        (chosen, chosen, shaped((cands, 1), jnp.int32)),
        [IN_SMEM] + [IN_VMEM] * 2,
    )(hist_lengths, codes, causal_offsets.T)

    taken = shaped((cands + slot_count, width))
    sent = call(pick_kernel, taken, [IN_VMEM] * 2)(choose_sent, gathered)
    came = lax.ppermute(sent, "seq", swap)
    kept, weight, keys, values = call(
        keep_kernel,
        (taken, shaped((width, width)), shaped((events, width)), shaped((events, width))),
        [IN_VMEM] * 2 + [IN_HBM] * 5,
        [pltpu.SemaphoreType.DMA((5,))],
    )(
        choose_kept,
        gathered,
        stay(hist_keys),
        stay(hist_values),
        stay(keys_far),
        stay(values_far),
        stay(proj_weight),
    )

    user_part, routed = call(
        attend_kernel,
        (shaped((cands, width)), shaped((cands + slot_count, width))),
        [IN_VMEM] * 6,
        vmem=48,
    )(kept, came, weight, seen, keys, values)
    backs = lax.all_to_all(
        user_part.reshape(devices, slot_count, width),
        "seq",
        split_axis=0,
        concat_axis=0,
        tiled=True,
        axis_index_groups=everyone,
    )

    own_mine = lax.dynamic_slice_in_dim(routed, mine_at * slot_count, slot_count, 0)
    own_other = routed[cands:]
    routed_own = jnp.where(
        core == 0,
        jnp.concatenate([own_mine, own_other]),
        jnp.concatenate([own_other, own_mine]),
    )
    proj = jax.nn.silu(jnp.dot(routed_own, proj_weight, preferred_element_type=jnp.float32))
    gate = proj[:, :width]
    value = proj[:, width : 2 * width].astype(jnp.bfloat16)
    query = proj[:, 2 * width : 3 * width].astype(jnp.bfloat16)
    key = proj[:, 3 * width :].astype(jnp.bfloat16)
    own = self_term(query, key, value)

    cand_out = call(
        finish_kernel, shaped((slot_count, users, width)), [IN_VMEM] * 5
    )(backs, own, gate, routed_own, out_weight)
    return (item_embed, cand_out)


def solution(mesh):
    return jax.shard_map(
        per_device,
        mesh=mesh,
        in_specs=(
            P(("grp", "seq"), None),
            P(),
            P(),
            P(),
            P(),
            P("grp", "seq", None),
            P("grp", "seq", None),
            P(("grp", "seq"), None, None),
            P(("grp", "seq"), None),
            P("grp"),
            P("grp", None),
        ),
        out_specs=(P(("grp", "seq"), None), P(("grp", "seq"), None, None)),
        check_vma=False,
    )
```

```python
import functools

import jax
import jax.numpy as jnp
from jax import lax
from jax.experimental import pallas as pl
from jax.experimental.pallas import tpu as pltpu
from jax.sharding import PartitionSpec as P


HEADS = 8
LANES = 128


def layer_norm(values):
    centre = values - jnp.mean(values, axis=-1, keepdims=True)
    return centre * lax.rsqrt(jnp.mean(centre * centre, axis=-1, keepdims=True) + 1e-05)


def self_term(query, key, value):
    rows, width = query.shape
    size = width // HEADS
    q_heads = query.astype(jnp.float32).reshape(rows, HEADS, size)
    k_heads = key.astype(jnp.float32).reshape(rows, HEADS, size)
    v_heads = value.astype(jnp.float32).reshape(rows, HEADS, size)
    score = jnp.sum(q_heads * k_heads, axis=-1) * size ** (-0.5)
    return (jax.nn.silu(score)[:, :, None] * v_heads).reshape(rows, width)


def ring_order(chips):
    ring = list(range(1, chips, 2)) + list(range(0, chips, 2))[::-1]
    start = ring.index(min(chips - 1, (chips // 2) | 1))
    return ring[start:] + ring[:start]


def middle_order(chips):
    return [(chips // 2 + step) % chips for step in range(chips)]


def place_in(order, chip):
    place = jnp.zeros_like(chip)
    for number, other in enumerate(order):
        place = jnp.where(chip == other, number, place)
    return place


def code_kernel(depth, rows, owner_hbm, row_hbm, out_ref, owner_ref, row_ref, sems):
    copies = (
        pltpu.make_async_copy(owner_hbm, owner_ref, sems.at[0]),
        pltpu.make_async_copy(row_hbm, row_ref, sems.at[1]),
    )
    for copy in copies:
        copy.start()
    for copy in copies:
        copy.wait()
    users = owner_ref.shape[0]
    owners = jnp.concatenate([owner_ref[user] for user in range(users)], axis=1)
    wanted = jnp.concatenate([row_ref[user : user + 1, :] for user in range(users)], axis=1)
    slots = owners.shape[1]
    before = lax.broadcasted_iota(jnp.int32, (slots, slots), 0) < lax.broadcasted_iota(
        jnp.int32, (slots, slots), 1
    )
    same = (column(owners, slots) == owners) & before
    ranks = jnp.sum(same.astype(jnp.int32), axis=0, keepdims=True)
    code = (owners * depth + ranks) * rows + wanted
    out_ref[...] = jnp.broadcast_to(code[None], out_ref.shape)


def asked_kernel(depth, codes_ref, embed_ref, out_hbm, chosen_ref, picked_ref, sems):
    devices, _, slots = codes_ref.shape
    rows = embed_ref.shape[0]
    want = lax.axis_index("seq") * depth + lax.broadcasted_iota(jnp.int32, (depth, slots), 0)
    lane = lax.broadcasted_iota(jnp.int32, (depth, rows), 1)
    copies = []
    parts = sems.shape[1]
    for part in range(parts):
        askers = range(devices * part // parts, devices * (part + 1) // parts)
        for asker in askers:
            codes = jnp.broadcast_to(codes_ref[asker], (depth, slots))
            hit = lax.div(codes, rows) == want
            asked = jnp.sum(jnp.where(hit, lax.rem(codes, rows), 0), axis=1, keepdims=True)
            chosen_ref[asker * depth : (asker + 1) * depth, :] = (lane == asked).astype(jnp.float32)
        span = slice(askers[0] * depth, (askers[-1] + 1) * depth)
        lines = pl.ds(askers[0] * depth, len(askers) * depth)
        picked_ref[span, :] = jnp.dot(
            chosen_ref[span, :].astype(jnp.bfloat16), embed_ref[...], preferred_element_type=jnp.float32
        ).astype(jnp.bfloat16)
        for receiver in range(out_hbm.shape[0]):
            copy = pltpu.make_async_copy(
                picked_ref.at[lines], out_hbm.at[receiver, lines], sems.at[receiver, part]
            )
            copy.start()
            copies.append(copy)
    for copy in copies:
        copy.wait()


def column(row, height):
    down = lax.broadcasted_iota(jnp.int32, (height, row.shape[1]), 0)
    along = lax.broadcasted_iota(jnp.int32, (height, row.shape[1]), 1)
    return jnp.sum(jnp.where(down == along, row, 0), axis=1, keepdims=True)


def ready_kernel(
    depth,
    rows,
    block,
    order,
    handing,
    lengths_ref,
    codes_ref,
    offsets_ref,
    sent_ref,
    kept_ref,
    seen_ref,
):
    devices, _, slots = codes_ref.shape
    users = offsets_ref.shape[0]
    slot_count = slots // users
    room = devices * depth
    me = lax.axis_index("seq")
    core = lax.rem(me, users)
    mine_at = place_in(order, lax.div(me, users)) * users + core
    asker = lax.broadcasted_iota(jnp.int32, codes_ref.shape, 0)
    places = lax.div(codes_ref[...], rows)
    owner = lax.div(places, depth)
    spots = jnp.where(
        lax.rem(owner, users) == core,
        place_in(handing, lax.div(owner, users)) * room + asker * depth + lax.rem(places, depth),
        -1,
    )
    first = spots[:, :, :slot_count]
    second = spots[:, :, slot_count:]
    mine = jnp.where(core == 0, first, second)
    other = jnp.where(core == 0, second, first)

    def one(array, index):
        return jnp.sum(jnp.where(asker[:, :, :slot_count] == index, array, 0), axis=0)

    cands = devices * slot_count
    blank = jnp.zeros((1, LANES - slot_count), jnp.int32)
    for chosen_ref, all_of, extra in (
        (sent_ref, other, one(mine, mine_at + 1 - 2 * core)),
        (kept_ref, mine, one(other, mine_at)),
    ):
        row = jnp.concatenate([all_of[r] for r in range(devices)] + [extra, blank], axis=1)
        spot = column(row, cands + slot_count)
        place = lax.broadcasted_iota(jnp.int32, chosen_ref.shape, 1)
        chosen_ref[...] = (place == spot).astype(jnp.float32).astype(jnp.bfloat16)

    offsets = jnp.where(core == 0, offsets_ref[0:1, :], offsets_ref[1:2, :])
    offsets = jnp.concatenate(
        [
            offsets[:, slot_count * device : slot_count * (device + 1)]
            for device in (users * chip + other for chip in order for other in range(users))
        ],
        axis=1,
    )
    seen_ref[...] = column(lengths_ref[core] - (me - core) * block - offsets, cands)


def pick_kernel(chosen_ref, gathered_ref, out_ref):
    out_ref[...] = jnp.dot(
        chosen_ref[...], gathered_ref[...], preferred_element_type=jnp.float32
    ).astype(out_ref.dtype)


def keep_kernel(
    chosen_ref,
    gathered_ref,
    keys_near,
    values_near,
    keys_far,
    values_far,
    proj_hbm,
    out_ref,
    weight_ref,
    keys_ref,
    values_ref,
    sems,
):
    users, block, width = keys_near.shape
    core = lax.rem(lax.axis_index("seq"), users)
    here = pl.ds(pl.multiple_of(core * block, block), block)
    there = pl.ds(pl.multiple_of((1 - core) * block, block), block)
    copies = (
        pltpu.make_async_copy(keys_near.at[core], keys_ref.at[here], sems.at[0]),
        pltpu.make_async_copy(values_near.at[core], values_ref.at[here], sems.at[1]),
        pltpu.make_async_copy(keys_far.at[core], keys_ref.at[there], sems.at[2]),
        pltpu.make_async_copy(values_far.at[core], values_ref.at[there], sems.at[3]),
        pltpu.make_async_copy(proj_hbm.at[:, pl.ds(2 * width, width)], weight_ref, sems.at[4]),
    )
    for copy in copies:
        copy.start()
    pick_kernel(chosen_ref, gathered_ref, out_ref)
    for copy in copies:
        copy.wait()


def attend_kernel(
    kept_ref, came_ref, weight_ref, seen_ref, keys, values, out_hbm, routed_ref, out_ref, sems
):
    rows, width = out_ref.shape
    size = width // HEADS
    routed = kept_ref[...] + came_ref[...]
    routed_ref[...] = routed
    query = jax.nn.silu(
        jnp.dot(routed[:rows], weight_ref[...], preferred_element_type=jnp.float32)
    ).astype(jnp.bfloat16)
    query = query * jnp.bfloat16(0.5 * size ** (-0.5))
    event = lax.broadcasted_iota(jnp.int32, (rows, keys.shape[0]), 1)
    shown = (event < seen_ref[...]).astype(jnp.float32).astype(jnp.bfloat16)
    lane = lax.broadcasted_iota(jnp.int32, (rows, LANES), 1)
    per_tile = LANES // size
    copies = []
    for tile in range(width // LANES):
        span = slice(tile * LANES, (tile + 1) * LANES)
        whole = query[:, span]
        joined = None
        for head in range(per_tile):
            mine = (lane >= head * size) & (lane < (head + 1) * size)
            part = jnp.where(mine, whole, jnp.zeros_like(whole))
            half = lax.dot_general(
                part, keys[:, span], (((1,), (1,)), ((), ())), preferred_element_type=jnp.float32
            ).astype(jnp.bfloat16)
            weight = half + half * jnp.tanh(half)
            weight = weight * shown
            total = jnp.dot(weight, values[:, span], preferred_element_type=jnp.float32)
            joined = total if joined is None else jnp.where(mine, total, joined)
        out_ref[:, span] = joined.astype(out_ref.dtype)
        copy = pltpu.make_async_copy(
            out_ref.at[:, pl.ds(tile * LANES, LANES)], out_hbm.at[:, pl.ds(tile * LANES, LANES)], sems.at[tile]
        )
        copy.start()
        copies.append(copy)
    for copy in copies:
        copy.wait()


def finish_kernel(backs_ref, own_ref, gate_ref, routed_ref, weight_ref, out_ref):
    slot_count, users, _ = out_ref.shape
    chips = backs_ref.shape[0] // users
    attended = []
    for user in range(users):
        parts = [backs_ref[chip * users + user].astype(jnp.float32) for chip in range(chips)]
        while len(parts) > 1:
            parts = [sum(parts[k : k + 2][1:], parts[k]) for k in range(0, len(parts), 2)]
        attended.append(parts[0])
    total = jnp.concatenate(attended, axis=0) + own_ref[...]
    mixed = (layer_norm(total) * gate_ref[...]).astype(jnp.bfloat16)
    result = routed_ref[...].astype(jnp.float32) + jnp.dot(
        mixed, weight_ref[...], preferred_element_type=jnp.float32
    )
    for cand in range(slot_count):
        rows = [result[user * slot_count + cand : user * slot_count + cand + 1] for user in range(users)]
        out_ref[cand] = jnp.concatenate(rows, axis=0).astype(out_ref.dtype)


IN_VMEM = pl.BlockSpec(memory_space=pltpu.VMEM)
IN_SMEM = pl.BlockSpec(memory_space=pltpu.SMEM)
IN_HBM = pl.BlockSpec(memory_space=pltpu.HBM)


def stay(array):
    return pltpu.with_memory_space_constraint(array, pltpu.HBM)


def call(kernel, outs, specs, scratch=(), vmem=24, out_space=IN_VMEM):
    many = isinstance(outs, tuple)
    return pl.pallas_call(
        kernel,
        out_shape=outs,
        in_specs=specs,
        out_specs=(out_space,) * len(outs) if many and not isinstance(out_space, tuple) else out_space,
        scratch_shapes=scratch,
        compiler_params=pltpu.CompilerParams(vmem_limit_bytes=vmem * 2**20),
    )


def shaped(shape, dtype=jnp.bfloat16):
    return jax.ShapeDtypeStruct(shape, dtype)


def per_device(
    item_features,
    tower_in,
    tower_out,
    proj_weight,
    out_weight,
    hist_keys,
    hist_values,
    owner_of,
    row_in,
    hist_lengths,
    causal_offsets,
):
    width = tower_out.shape[1]
    devices = lax.axis_size("seq")
    me = lax.axis_index("seq")
    slot_count, users = row_in.shape
    assert users == 2 and devices % users == 0
    slots = slot_count * users
    rows = item_features.shape[0]
    hist_dev = hist_keys.shape[1]
    depth = max(2, 2 * slots // devices)
    room = devices * depth
    core = me % users
    swap = [(i, i ^ 1) for i in range(devices)]
    half = devices // users
    order = ring_order(half)
    handing = middle_order(half)
    everyone = [[users * chip + other for chip in order for other in range(users)]]
    alike = [[users * chip + other for chip in handing] for other in range(users)]
    mine_at = place_in(order, me // users) * users + core
    cands = devices * slot_count

    codes = lax.all_to_all(
        call(
            functools.partial(code_kernel, depth, rows),
            shaped((devices, 1, slots), jnp.int32),
            [IN_HBM] * 2,
            [
                pltpu.VMEM((users, 1, slot_count), jnp.int32),
                pltpu.VMEM((users, slot_count), jnp.int32),
                pltpu.SemaphoreType.DMA((2,)),
            ],
        )(stay(owner_of.transpose(1, 2, 0)), stay(row_in.T)),
        "seq",
        split_axis=0,
        concat_axis=0,
        tiled=True,
        axis_index_groups=everyone,
    )

    keys_far = lax.ppermute(hist_keys, "seq", swap)
    values_far = lax.ppermute(hist_values, "seq", swap)

    hidden = jax.nn.silu(
        jnp.dot(item_features, tower_in, preferred_element_type=jnp.float32)
    ).astype(jnp.bfloat16)
    item_embed = jnp.dot(hidden, tower_out, preferred_element_type=jnp.float32).astype(jnp.bfloat16)

    handed = call(
        functools.partial(asked_kernel, depth),
        shaped((half, room, width)),
        [IN_VMEM] * 2,
        [
            pltpu.VMEM((room, rows), jnp.float32),
            pltpu.VMEM((room, width), jnp.bfloat16),
            pltpu.SemaphoreType.DMA((half, 1)),
        ],
        out_space=IN_HBM,
    )(codes, item_embed)
    gathered = lax.all_to_all(
        handed, "seq", split_axis=0, concat_axis=0, tiled=True, axis_index_groups=alike
    )
    gathered = gathered.reshape(half * room, width)

    chosen = shaped((cands + slot_count, half * room))
    events = users * hist_dev
    choose_sent, choose_kept, seen = call(
        functools.partial(ready_kernel, depth, rows, hist_dev, order, handing),
        (chosen, chosen, shaped((cands, 1), jnp.int32)),
        [IN_SMEM] + [IN_VMEM] * 2,
    )(hist_lengths, codes, causal_offsets.T)

    taken = shaped((cands + slot_count, width))
    sent = call(pick_kernel, taken, [IN_VMEM] * 2)(choose_sent, gathered)
    came = lax.ppermute(sent, "seq", swap)
    kept, weight, keys, values = call(
        keep_kernel,
        (taken, shaped((width, width)), shaped((events, width)), shaped((events, width))),
        [IN_VMEM] * 2 + [IN_HBM] * 5,
        [pltpu.SemaphoreType.DMA((5,))],
    )(
        choose_kept,
        gathered,
        stay(hist_keys),
        stay(hist_values),
        stay(keys_far),
        stay(values_far),
        stay(proj_weight),
    )

    user_part, routed = call(
        attend_kernel,
        (shaped((cands, width)), shaped((cands + slot_count, width))),
        [IN_VMEM] * 6,
        [pltpu.VMEM((cands, width), jnp.bfloat16), pltpu.SemaphoreType.DMA((width // LANES,))],
        vmem=48,
        out_space=(IN_HBM, IN_VMEM),
    )(kept, came, weight, seen, keys, values)
    backs = lax.all_to_all(
        user_part.reshape(devices, slot_count, width),
        "seq",
        split_axis=0,
        concat_axis=0,
        tiled=True,
        axis_index_groups=everyone,
    )

    own_mine = lax.dynamic_slice_in_dim(routed, mine_at * slot_count, slot_count, 0)
    own_other = routed[cands:]
    routed_own = jnp.where(
        core == 0,
        jnp.concatenate([own_mine, own_other]),
        jnp.concatenate([own_other, own_mine]),
    )
    proj = jax.nn.silu(jnp.dot(routed_own, proj_weight, preferred_element_type=jnp.float32))
    gate = proj[:, :width]
    value = proj[:, width : 2 * width].astype(jnp.bfloat16)
    query = proj[:, 2 * width : 3 * width].astype(jnp.bfloat16)
    key = proj[:, 3 * width :].astype(jnp.bfloat16)
    own = self_term(query, key, value)

    cand_out = call(
        finish_kernel, shaped((slot_count, users, width)), [IN_VMEM] * 5
    )(backs, own, gate, routed_own, out_weight)
    return (item_embed, cand_out)


def solution(mesh):
    return jax.shard_map(
        per_device,
        mesh=mesh,
        in_specs=(
            P(("grp", "seq"), None),
            P(),
            P(),
            P(),
            P(),
            P("grp", "seq", None),
            P("grp", "seq", None),
            P(("grp", "seq"), None, None),
            P(("grp", "seq"), None),
            P("grp"),
            P("grp", None),
        ),
        out_specs=(P(("grp", "seq"), None), P(("grp", "seq"), None, None)),
        check_vma=False,
    )
```

```python
import functools

import jax
import jax.numpy as jnp
from jax import lax
from jax.experimental import pallas as pl
from jax.experimental.pallas import tpu as pltpu
from jax.sharding import PartitionSpec as P


HEADS = 8
LANES = 128


def layer_norm(values):
    centre = values - jnp.mean(values, axis=-1, keepdims=True)
    return centre * lax.rsqrt(jnp.mean(centre * centre, axis=-1, keepdims=True) + 1e-05)


def self_term(query, key, value):
    rows, width = query.shape
    size = width // HEADS
    q_heads = query.astype(jnp.float32).reshape(rows, HEADS, size)
    k_heads = key.astype(jnp.float32).reshape(rows, HEADS, size)
    v_heads = value.astype(jnp.float32).reshape(rows, HEADS, size)
    score = jnp.sum(q_heads * k_heads, axis=-1) * size ** (-0.5)
    return (jax.nn.silu(score)[:, :, None] * v_heads).reshape(rows, width)


def ring_order(chips):
    ring = list(range(1, chips, 2)) + list(range(0, chips, 2))[::-1]
    start = ring.index(min(chips - 1, (chips // 2) | 1))
    return ring[start:] + ring[:start]


def middle_order(chips):
    return [(chips // 2 + step) % chips for step in range(chips)]


def place_in(order, chip):
    place = jnp.zeros_like(chip)
    for number, other in enumerate(order):
        place = jnp.where(chip == other, number, place)
    return place


def code_kernel(depth, rows, owner_hbm, row_hbm, out_ref, owner_ref, row_ref, sems):
    copies = (
        pltpu.make_async_copy(owner_hbm, owner_ref, sems.at[0]),
        pltpu.make_async_copy(row_hbm, row_ref, sems.at[1]),
    )
    for copy in copies:
        copy.start()
    for copy in copies:
        copy.wait()
    users = owner_ref.shape[0]
    owners = jnp.concatenate([owner_ref[user] for user in range(users)], axis=1)
    wanted = jnp.concatenate([row_ref[user : user + 1, :] for user in range(users)], axis=1)
    slots = owners.shape[1]
    before = lax.broadcasted_iota(jnp.int32, (slots, slots), 0) < lax.broadcasted_iota(
        jnp.int32, (slots, slots), 1
    )
    same = (column(owners, slots) == owners) & before
    ranks = jnp.sum(same.astype(jnp.int32), axis=0, keepdims=True)
    code = (owners * depth + ranks) * rows + wanted
    out_ref[...] = jnp.broadcast_to(code[None], out_ref.shape)


def asked_kernel(depth, codes_ref, embed_ref, out_hbm, chosen_ref, picked_ref, sems):
    devices, _, slots = codes_ref.shape
    rows = embed_ref.shape[0]
    want = lax.axis_index("seq") * depth + lax.broadcasted_iota(jnp.int32, (depth, slots), 0)
    lane = lax.broadcasted_iota(jnp.int32, (depth, rows), 1)
    copies = []
    parts = sems.shape[1]
    for part in range(parts):
        askers = range(devices * part // parts, devices * (part + 1) // parts)
        for asker in askers:
            codes = jnp.broadcast_to(codes_ref[asker], (depth, slots))
            inside = codes - want * rows
            asked = jnp.sum(
                jnp.where((inside >= 0) & (inside < rows), inside, 0), axis=1, keepdims=True
            )
            chosen_ref[asker * depth : (asker + 1) * depth, :] = (lane == asked).astype(jnp.float32)
        span = slice(askers[0] * depth, (askers[-1] + 1) * depth)
        lines = pl.ds(askers[0] * depth, len(askers) * depth)
        picked_ref[span, :] = jnp.dot(
            chosen_ref[span, :].astype(jnp.bfloat16), embed_ref[...], preferred_element_type=jnp.float32
        ).astype(jnp.bfloat16)
        for receiver in range(out_hbm.shape[0]):
            copy = pltpu.make_async_copy(
                picked_ref.at[lines], out_hbm.at[receiver, lines], sems.at[receiver, part]
            )
            copy.start()
            copies.append(copy)
    for copy in copies:
        copy.wait()


def column(row, height):
    down = lax.broadcasted_iota(jnp.int32, (height, row.shape[1]), 0)
    along = lax.broadcasted_iota(jnp.int32, (height, row.shape[1]), 1)
    return jnp.sum(jnp.where(down == along, row, 0), axis=1, keepdims=True)


def ready_kernel(
    depth,
    rows,
    block,
    order,
    handing,
    lengths_ref,
    codes_ref,
    offsets_ref,
    sent_ref,
    kept_ref,
    seen_ref,
):
    devices, _, slots = codes_ref.shape
    users = offsets_ref.shape[0]
    slot_count = slots // users
    room = devices * depth
    me = lax.axis_index("seq")
    core = lax.rem(me, users)
    mine_at = place_in(order, lax.div(me, users)) * users + core
    asker = lax.broadcasted_iota(jnp.int32, codes_ref.shape, 0)
    places = lax.div(codes_ref[...], rows)
    owner = lax.div(places, depth)
    spots = jnp.where(
        lax.rem(owner, users) == core,
        place_in(handing, lax.div(owner, users)) * room + asker * depth + lax.rem(places, depth),
        -1,
    )
    first = spots[:, :, :slot_count]
    second = spots[:, :, slot_count:]
    mine = jnp.where(core == 0, first, second)
    other = jnp.where(core == 0, second, first)

    def one(array, index):
        return jnp.sum(jnp.where(asker[:, :, :slot_count] == index, array, 0), axis=0)

    cands = devices * slot_count
    blank = jnp.zeros((1, LANES - slot_count), jnp.int32)
    for chosen_ref, all_of, extra in (
        (sent_ref, other, one(mine, mine_at + 1 - 2 * core)),
        (kept_ref, mine, one(other, mine_at)),
    ):
        row = jnp.concatenate([all_of[r] for r in range(devices)] + [extra, blank], axis=1)
        spot = column(row, cands + slot_count)
        place = lax.broadcasted_iota(jnp.int32, chosen_ref.shape, 1)
        chosen_ref[...] = (place == spot).astype(jnp.float32).astype(jnp.bfloat16)

    offsets = jnp.where(core == 0, offsets_ref[0:1, :], offsets_ref[1:2, :])
    offsets = jnp.concatenate(
        [
            offsets[:, slot_count * device : slot_count * (device + 1)]
            for device in (users * chip + other for chip in order for other in range(users))
        ],
        axis=1,
    )
    seen_ref[...] = column(lengths_ref[core] - (me - core) * block - offsets, cands)


def pick_kernel(chosen_ref, gathered_ref, out_ref):
    out_ref[...] = jnp.dot(
        chosen_ref[...], gathered_ref[...], preferred_element_type=jnp.float32
    ).astype(out_ref.dtype)


def keep_kernel(
    chosen_ref,
    gathered_ref,
    keys_near,
    values_near,
    keys_far,
    values_far,
    proj_hbm,
    out_ref,
    weight_ref,
    keys_ref,
    values_ref,
    sems,
):
    users, block, width = keys_near.shape
    core = lax.rem(lax.axis_index("seq"), users)
    here = pl.ds(pl.multiple_of(core * block, block), block)
    there = pl.ds(pl.multiple_of((1 - core) * block, block), block)
    copies = (
        pltpu.make_async_copy(keys_near.at[core], keys_ref.at[here], sems.at[0]),
        pltpu.make_async_copy(values_near.at[core], values_ref.at[here], sems.at[1]),
        pltpu.make_async_copy(keys_far.at[core], keys_ref.at[there], sems.at[2]),
        pltpu.make_async_copy(values_far.at[core], values_ref.at[there], sems.at[3]),
        pltpu.make_async_copy(proj_hbm.at[:, pl.ds(2 * width, width)], weight_ref, sems.at[4]),
    )
    for copy in copies:
        copy.start()
    pick_kernel(chosen_ref, gathered_ref, out_ref)
    for copy in copies:
        copy.wait()


def attend_kernel(
    kept_ref, came_ref, weight_ref, seen_ref, keys, values, out_hbm, routed_ref, out_ref, sems
):
    rows, width = out_ref.shape
    size = width // HEADS
    routed = kept_ref[...] + came_ref[...]
    routed_ref[...] = routed
    query = jax.nn.silu(
        jnp.dot(routed[:rows], weight_ref[...], preferred_element_type=jnp.float32)
    ).astype(jnp.bfloat16)
    query = query * jnp.bfloat16(0.5 * size ** (-0.5))
    event = lax.broadcasted_iota(jnp.int32, (rows, keys.shape[0]), 1)
    shown = (event < seen_ref[...]).astype(jnp.float32).astype(jnp.bfloat16)
    lane = lax.broadcasted_iota(jnp.int32, (rows, LANES), 1)
    per_tile = LANES // size
    copies = []
    for tile in range(width // LANES):
        span = slice(tile * LANES, (tile + 1) * LANES)
        whole = query[:, span]
        joined = None
        for head in range(per_tile):
            mine = (lane >= head * size) & (lane < (head + 1) * size)
            part = jnp.where(mine, whole, jnp.zeros_like(whole))
            half = lax.dot_general(
                part, keys[:, span], (((1,), (1,)), ((), ())), preferred_element_type=jnp.float32
            ).astype(jnp.bfloat16)
            weight = half + half * jnp.tanh(half)
            weight = weight * shown
            total = jnp.dot(weight, values[:, span], preferred_element_type=jnp.float32)
            joined = total if joined is None else jnp.where(mine, total, joined)
        out_ref[:, span] = joined.astype(out_ref.dtype)
        copy = pltpu.make_async_copy(
            out_ref.at[:, pl.ds(tile * LANES, LANES)], out_hbm.at[:, pl.ds(tile * LANES, LANES)], sems.at[tile]
        )
        copy.start()
        copies.append(copy)
    for copy in copies:
        copy.wait()


def finish_kernel(backs_ref, own_ref, gate_ref, routed_ref, weight_ref, out_ref):
    slot_count, users, _ = out_ref.shape
    chips = backs_ref.shape[0] // users
    attended = []
    for user in range(users):
        parts = [backs_ref[chip * users + user].astype(jnp.float32) for chip in range(chips)]
        while len(parts) > 1:
            parts = [sum(parts[k : k + 2][1:], parts[k]) for k in range(0, len(parts), 2)]
        attended.append(parts[0])
    total = jnp.concatenate(attended, axis=0) + own_ref[...]
    mixed = (layer_norm(total) * gate_ref[...]).astype(jnp.bfloat16)
    result = routed_ref[...].astype(jnp.float32) + jnp.dot(
        mixed, weight_ref[...], preferred_element_type=jnp.float32
    )
    for cand in range(slot_count):
        rows = [result[user * slot_count + cand : user * slot_count + cand + 1] for user in range(users)]
        out_ref[cand] = jnp.concatenate(rows, axis=0).astype(out_ref.dtype)


IN_VMEM = pl.BlockSpec(memory_space=pltpu.VMEM)
IN_SMEM = pl.BlockSpec(memory_space=pltpu.SMEM)
IN_HBM = pl.BlockSpec(memory_space=pltpu.HBM)


def stay(array):
    return pltpu.with_memory_space_constraint(array, pltpu.HBM)


def call(kernel, outs, specs, scratch=(), vmem=24, out_space=IN_VMEM):
    many = isinstance(outs, tuple)
    return pl.pallas_call(
        kernel,
        out_shape=outs,
        in_specs=specs,
        out_specs=(out_space,) * len(outs) if many and not isinstance(out_space, tuple) else out_space,
        scratch_shapes=scratch,
        compiler_params=pltpu.CompilerParams(vmem_limit_bytes=vmem * 2**20),
    )


def shaped(shape, dtype=jnp.bfloat16):
    return jax.ShapeDtypeStruct(shape, dtype)


def per_device(
    item_features,
    tower_in,
    tower_out,
    proj_weight,
    out_weight,
    hist_keys,
    hist_values,
    owner_of,
    row_in,
    hist_lengths,
    causal_offsets,
):
    width = tower_out.shape[1]
    devices = lax.axis_size("seq")
    me = lax.axis_index("seq")
    slot_count, users = row_in.shape
    assert users == 2 and devices % users == 0
    slots = slot_count * users
    rows = item_features.shape[0]
    hist_dev = hist_keys.shape[1]
    depth = max(2, 2 * slots // devices)
    room = devices * depth
    core = me % users
    swap = [(i, i ^ 1) for i in range(devices)]
    half = devices // users
    order = ring_order(half)
    handing = middle_order(half)
    everyone = [[users * chip + other for chip in order for other in range(users)]]
    alike = [[users * chip + other for chip in handing] for other in range(users)]
    mine_at = place_in(order, me // users) * users + core
    cands = devices * slot_count

    codes = lax.all_to_all(
        call(
            functools.partial(code_kernel, depth, rows),
            shaped((devices, 1, slots), jnp.int32),
            [IN_HBM] * 2,
            [
                pltpu.VMEM((users, 1, slot_count), jnp.int32),
                pltpu.VMEM((users, slot_count), jnp.int32),
                pltpu.SemaphoreType.DMA((2,)),
            ],
        )(stay(owner_of.transpose(1, 2, 0)), stay(row_in.T)),
        "seq",
        split_axis=0,
        concat_axis=0,
        tiled=True,
        axis_index_groups=everyone,
    )

    keys_far = lax.ppermute(hist_keys, "seq", swap)
    values_far = lax.ppermute(hist_values, "seq", swap)

    hidden = jax.nn.silu(
        jnp.dot(item_features, tower_in, preferred_element_type=jnp.float32)
    ).astype(jnp.bfloat16)
    item_embed = jnp.dot(hidden, tower_out, preferred_element_type=jnp.float32).astype(jnp.bfloat16)

    handed = call(
        functools.partial(asked_kernel, depth),
        shaped((half, room, width)),
        [IN_VMEM] * 2,
        [
            pltpu.VMEM((room, rows), jnp.float32),
            pltpu.VMEM((room, width), jnp.bfloat16),
            pltpu.SemaphoreType.DMA((half, 1)),
        ],
        out_space=IN_HBM,
    )(codes, item_embed)
    gathered = lax.all_to_all(
        handed, "seq", split_axis=0, concat_axis=0, tiled=True, axis_index_groups=alike
    )
    gathered = gathered.reshape(half * room, width)

    chosen = shaped((cands + slot_count, half * room))
    events = users * hist_dev
    choose_sent, choose_kept, seen = call(
        functools.partial(ready_kernel, depth, rows, hist_dev, order, handing),
        (chosen, chosen, shaped((cands, 1), jnp.int32)),
        [IN_SMEM] + [IN_VMEM] * 2,
    )(hist_lengths, codes, causal_offsets.T)

    taken = shaped((cands + slot_count, width))
    sent = call(pick_kernel, taken, [IN_VMEM] * 2)(choose_sent, gathered)
    came = lax.ppermute(sent, "seq", swap)
    kept, weight, keys, values = call(
        keep_kernel,
        (taken, shaped((width, width)), shaped((events, width)), shaped((events, width))),
        [IN_VMEM] * 2 + [IN_HBM] * 5,
        [pltpu.SemaphoreType.DMA((5,))],
    )(
        choose_kept,
        gathered,
        stay(hist_keys),
        stay(hist_values),
        stay(keys_far),
        stay(values_far),
        stay(proj_weight),
    )

    user_part, routed = call(
        attend_kernel,
        (shaped((cands, width)), shaped((cands + slot_count, width))),
        [IN_VMEM] * 6,
        [pltpu.VMEM((cands, width), jnp.bfloat16), pltpu.SemaphoreType.DMA((width // LANES,))],
        vmem=48,
        out_space=(IN_HBM, IN_VMEM),
    )(kept, came, weight, seen, keys, values)
    backs = lax.all_to_all(
        user_part.reshape(devices, slot_count, width),
        "seq",
        split_axis=0,
        concat_axis=0,
        tiled=True,
        axis_index_groups=everyone,
    )

    own_mine = lax.dynamic_slice_in_dim(routed, mine_at * slot_count, slot_count, 0)
    own_other = routed[cands:]
    routed_own = jnp.where(
        core == 0,
        jnp.concatenate([own_mine, own_other]),
        jnp.concatenate([own_other, own_mine]),
    )
    proj = jax.nn.silu(jnp.dot(routed_own, proj_weight, preferred_element_type=jnp.float32))
    gate = proj[:, :width]
    value = proj[:, width : 2 * width].astype(jnp.bfloat16)
    query = proj[:, 2 * width : 3 * width].astype(jnp.bfloat16)
    key = proj[:, 3 * width :].astype(jnp.bfloat16)
    own = self_term(query, key, value)

    cand_out = call(
        finish_kernel, shaped((slot_count, users, width)), [IN_VMEM] * 5
    )(backs, own, gate, routed_own, out_weight)
    return (item_embed, cand_out)


def solution(mesh):
    return jax.shard_map(
        per_device,
        mesh=mesh,
        in_specs=(
            P(("grp", "seq"), None),
            P(),
            P(),
            P(),
            P(),
            P("grp", "seq", None),
            P("grp", "seq", None),
            P(("grp", "seq"), None, None),
            P(("grp", "seq"), None),
            P("grp"),
            P("grp", None),
        ),
        out_specs=(P(("grp", "seq"), None), P(("grp", "seq"), None, None)),
        check_vma=False,
    )
```

```python
import functools

import jax
import jax.numpy as jnp
from jax import lax
from jax.experimental import pallas as pl
from jax.experimental.pallas import tpu as pltpu
from jax.sharding import PartitionSpec as P


HEADS = 8
LANES = 128


def layer_norm(values):
    centre = values - jnp.mean(values, axis=-1, keepdims=True)
    return centre * lax.rsqrt(jnp.mean(centre * centre, axis=-1, keepdims=True) + 1e-05)


def self_term(query, key, value):
    rows, width = query.shape
    size = width // HEADS
    q_heads = query.astype(jnp.float32).reshape(rows, HEADS, size)
    k_heads = key.astype(jnp.float32).reshape(rows, HEADS, size)
    v_heads = value.astype(jnp.float32).reshape(rows, HEADS, size)
    score = jnp.sum(q_heads * k_heads, axis=-1) * size ** (-0.5)
    return (jax.nn.silu(score)[:, :, None] * v_heads).reshape(rows, width)


def ring_order(chips):
    half = chips // 2
    ring = list(range(1, half, 2)) + list(range(0, half, 2))[::-1]
    return [half + chip for chip in ring] + ring[:1] + ring[:0:-1] + list(range(2 * half, chips))


def middle_order(chips):
    return [(chips // 2 + step) % chips for step in range(chips)]


def place_in(order, chip):
    place = jnp.zeros_like(chip)
    for number, other in enumerate(order):
        place = jnp.where(chip == other, number, place)
    return place


def code_kernel(depth, rows, owner_hbm, row_hbm, out_ref, owner_ref, row_ref, sems):
    copies = (
        pltpu.make_async_copy(owner_hbm, owner_ref, sems.at[0]),
        pltpu.make_async_copy(row_hbm, row_ref, sems.at[1]),
    )
    for copy in copies:
        copy.start()
    for copy in copies:
        copy.wait()
    users = owner_ref.shape[0]
    owners = jnp.concatenate([owner_ref[user] for user in range(users)], axis=1)
    wanted = jnp.concatenate([row_ref[user : user + 1, :] for user in range(users)], axis=1)
    slots = owners.shape[1]
    before = lax.broadcasted_iota(jnp.int32, (slots, slots), 0) < lax.broadcasted_iota(
        jnp.int32, (slots, slots), 1
    )
    same = (column(owners, slots) == owners) & before
    ranks = jnp.sum(same.astype(jnp.int32), axis=0, keepdims=True)
    code = (owners * depth + ranks) * rows + wanted
    out_ref[...] = jnp.broadcast_to(code[None], out_ref.shape)


def asked_kernel(depth, codes_ref, embed_ref, out_hbm, chosen_ref, picked_ref, sems):
    devices, _, slots = codes_ref.shape
    rows = embed_ref.shape[0]
    want = lax.axis_index("seq") * depth + lax.broadcasted_iota(jnp.int32, (depth, slots), 0)
    lane = lax.broadcasted_iota(jnp.int32, (depth, rows), 1)
    copies = []
    parts = sems.shape[1]
    for part in range(parts):
        askers = range(devices * part // parts, devices * (part + 1) // parts)
        for asker in askers:
            codes = jnp.broadcast_to(codes_ref[asker], (depth, slots))
            hit = lax.div(codes, rows) == want
            asked = jnp.sum(jnp.where(hit, lax.rem(codes, rows), 0), axis=1, keepdims=True)
            chosen_ref[asker * depth : (asker + 1) * depth, :] = (lane == asked).astype(jnp.float32)
        span = slice(askers[0] * depth, (askers[-1] + 1) * depth)
        lines = pl.ds(askers[0] * depth, len(askers) * depth)
        picked_ref[span, :] = jnp.dot(
            chosen_ref[span, :].astype(jnp.bfloat16), embed_ref[...], preferred_element_type=jnp.float32
        ).astype(jnp.bfloat16)
        for receiver in range(out_hbm.shape[0]):
            copy = pltpu.make_async_copy(
                picked_ref.at[lines], out_hbm.at[receiver, lines], sems.at[receiver, part]
            )
            copy.start()
            copies.append(copy)
    for copy in copies:
        copy.wait()


def column(row, height):
    down = lax.broadcasted_iota(jnp.int32, (height, row.shape[1]), 0)
    along = lax.broadcasted_iota(jnp.int32, (height, row.shape[1]), 1)
    return jnp.sum(jnp.where(down == along, row, 0), axis=1, keepdims=True)


def ready_kernel(
    depth,
    rows,
    block,
    order,
    handing,
    lengths_ref,
    codes_ref,
    offsets_ref,
    sent_ref,
    kept_ref,
    seen_ref,
):
    devices, _, slots = codes_ref.shape
    users = offsets_ref.shape[0]
    slot_count = slots // users
    room = devices * depth
    me = lax.axis_index("seq")
    core = lax.rem(me, users)
    mine_at = place_in(order, lax.div(me, users)) * users + core
    asker = lax.broadcasted_iota(jnp.int32, codes_ref.shape, 0)
    places = lax.div(codes_ref[...], rows)
    owner = lax.div(places, depth)
    spots = jnp.where(
        lax.rem(owner, users) == core,
        place_in(handing, lax.div(owner, users)) * room + asker * depth + lax.rem(places, depth),
        -1,
    )
    first = spots[:, :, :slot_count]
    second = spots[:, :, slot_count:]
    mine = jnp.where(core == 0, first, second)
    other = jnp.where(core == 0, second, first)

    def one(array, index):
        return jnp.sum(jnp.where(asker[:, :, :slot_count] == index, array, 0), axis=0)

    cands = devices * slot_count
    blank = jnp.zeros((1, LANES - slot_count), jnp.int32)
    for chosen_ref, all_of, extra in (
        (sent_ref, other, one(mine, mine_at + 1 - 2 * core)),
        (kept_ref, mine, one(other, mine_at)),
    ):
        row = jnp.concatenate([all_of[r] for r in range(devices)] + [extra, blank], axis=1)
        spot = column(row, cands + slot_count)
        place = lax.broadcasted_iota(jnp.int32, chosen_ref.shape, 1)
        chosen_ref[...] = (place == spot).astype(jnp.float32).astype(jnp.bfloat16)

    offsets = jnp.where(core == 0, offsets_ref[0:1, :], offsets_ref[1:2, :])
    offsets = jnp.concatenate(
        [
            offsets[:, slot_count * device : slot_count * (device + 1)]
            for device in (users * chip + other for chip in order for other in range(users))
        ],
        axis=1,
    )
    seen_ref[...] = column(lengths_ref[core] - (me - core) * block - offsets, cands)


def pick_kernel(chosen_ref, gathered_ref, out_ref):
    out_ref[...] = jnp.dot(
        chosen_ref[...], gathered_ref[...], preferred_element_type=jnp.float32
    ).astype(out_ref.dtype)


def keep_kernel(
    chosen_ref,
    gathered_ref,
    keys_near,
    values_near,
    keys_far,
    values_far,
    proj_hbm,
    out_ref,
    weight_ref,
    keys_ref,
    values_ref,
    sems,
):
    users, block, width = keys_near.shape
    core = lax.rem(lax.axis_index("seq"), users)
    here = pl.ds(pl.multiple_of(core * block, block), block)
    there = pl.ds(pl.multiple_of((1 - core) * block, block), block)
    copies = (
        pltpu.make_async_copy(keys_near.at[core], keys_ref.at[here], sems.at[0]),
        pltpu.make_async_copy(values_near.at[core], values_ref.at[here], sems.at[1]),
        pltpu.make_async_copy(keys_far.at[core], keys_ref.at[there], sems.at[2]),
        pltpu.make_async_copy(values_far.at[core], values_ref.at[there], sems.at[3]),
        pltpu.make_async_copy(proj_hbm.at[:, pl.ds(2 * width, width)], weight_ref, sems.at[4]),
    )
    for copy in copies:
        copy.start()
    pick_kernel(chosen_ref, gathered_ref, out_ref)
    for copy in copies:
        copy.wait()


def attend_kernel(
    kept_ref, came_ref, weight_ref, seen_ref, keys, values, out_hbm, routed_ref, out_ref, sems
):
    rows, width = out_ref.shape
    size = width // HEADS
    routed = kept_ref[...] + came_ref[...]
    routed_ref[...] = routed
    query = jax.nn.silu(
        jnp.dot(routed[:rows], weight_ref[...], preferred_element_type=jnp.float32)
    ).astype(jnp.bfloat16)
    query = query * jnp.bfloat16(0.5 * size ** (-0.5))
    event = lax.broadcasted_iota(jnp.int32, (rows, keys.shape[0]), 1)
    shown = (event < seen_ref[...]).astype(jnp.float32).astype(jnp.bfloat16)
    lane = lax.broadcasted_iota(jnp.int32, (rows, LANES), 1)
    per_tile = LANES // size
    copies = []
    for tile in range(width // LANES):
        span = slice(tile * LANES, (tile + 1) * LANES)
        whole = query[:, span]
        joined = None
        for head in range(per_tile):
            mine = (lane >= head * size) & (lane < (head + 1) * size)
            part = jnp.where(mine, whole, jnp.zeros_like(whole))
            half = lax.dot_general(
                part, keys[:, span], (((1,), (1,)), ((), ())), preferred_element_type=jnp.float32
            ).astype(jnp.bfloat16)
            weight = half + half * jnp.tanh(half)
            weight = weight * shown
            total = jnp.dot(weight, values[:, span], preferred_element_type=jnp.float32)
            joined = total if joined is None else jnp.where(mine, total, joined)
        out_ref[:, span] = joined.astype(out_ref.dtype)
        copy = pltpu.make_async_copy(
            out_ref.at[:, pl.ds(tile * LANES, LANES)], out_hbm.at[:, pl.ds(tile * LANES, LANES)], sems.at[tile]
        )
        copy.start()
        copies.append(copy)
    for copy in copies:
        copy.wait()


def finish_kernel(backs_ref, own_ref, gate_ref, routed_ref, weight_ref, out_ref):
    slot_count, users, _ = out_ref.shape
    chips = backs_ref.shape[0] // users
    attended = []
    for user in range(users):
        parts = [backs_ref[chip * users + user].astype(jnp.float32) for chip in range(chips)]
        while len(parts) > 1:
            parts = [sum(parts[k : k + 2][1:], parts[k]) for k in range(0, len(parts), 2)]
        attended.append(parts[0])
    total = jnp.concatenate(attended, axis=0) + own_ref[...]
    mixed = (layer_norm(total) * gate_ref[...]).astype(jnp.bfloat16)
    result = routed_ref[...].astype(jnp.float32) + jnp.dot(
        mixed, weight_ref[...], preferred_element_type=jnp.float32
    )
    for cand in range(slot_count):
        rows = [result[user * slot_count + cand : user * slot_count + cand + 1] for user in range(users)]
        out_ref[cand] = jnp.concatenate(rows, axis=0).astype(out_ref.dtype)


IN_VMEM = pl.BlockSpec(memory_space=pltpu.VMEM)
IN_SMEM = pl.BlockSpec(memory_space=pltpu.SMEM)
IN_HBM = pl.BlockSpec(memory_space=pltpu.HBM)


def stay(array):
    return pltpu.with_memory_space_constraint(array, pltpu.HBM)


def call(kernel, outs, specs, scratch=(), vmem=24, out_space=IN_VMEM):
    many = isinstance(outs, tuple)
    return pl.pallas_call(
        kernel,
        out_shape=outs,
        in_specs=specs,
        out_specs=(out_space,) * len(outs) if many and not isinstance(out_space, tuple) else out_space,
        scratch_shapes=scratch,
        compiler_params=pltpu.CompilerParams(vmem_limit_bytes=vmem * 2**20),
    )


def shaped(shape, dtype=jnp.bfloat16):
    return jax.ShapeDtypeStruct(shape, dtype)


def per_device(
    item_features,
    tower_in,
    tower_out,
    proj_weight,
    out_weight,
    hist_keys,
    hist_values,
    owner_of,
    row_in,
    hist_lengths,
    causal_offsets,
):
    width = tower_out.shape[1]
    devices = lax.axis_size("seq")
    me = lax.axis_index("seq")
    slot_count, users = row_in.shape
    assert users == 2 and devices % users == 0
    slots = slot_count * users
    rows = item_features.shape[0]
    hist_dev = hist_keys.shape[1]
    depth = max(2, 2 * slots // devices)
    room = devices * depth
    core = me % users
    swap = [(i, i ^ 1) for i in range(devices)]
    half = devices // users
    order = ring_order(half)
    handing = middle_order(half)
    everyone = [[users * chip + other for chip in order for other in range(users)]]
    alike = [[users * chip + other for chip in handing] for other in range(users)]
    mine_at = place_in(order, me // users) * users + core
    cands = devices * slot_count

    codes = lax.all_to_all(
        call(
            functools.partial(code_kernel, depth, rows),
            shaped((devices, 1, slots), jnp.int32),
            [IN_HBM] * 2,
            [
                pltpu.VMEM((users, 1, slot_count), jnp.int32),
                pltpu.VMEM((users, slot_count), jnp.int32),
                pltpu.SemaphoreType.DMA((2,)),
            ],
        )(stay(owner_of.transpose(1, 2, 0)), stay(row_in.T)),
        "seq",
        split_axis=0,
        concat_axis=0,
        tiled=True,
        axis_index_groups=everyone,
    )

    keys_far = lax.ppermute(hist_keys, "seq", swap)
    values_far = lax.ppermute(hist_values, "seq", swap)

    hidden = jax.nn.silu(
        jnp.dot(item_features, tower_in, preferred_element_type=jnp.float32)
    ).astype(jnp.bfloat16)
    item_embed = jnp.dot(hidden, tower_out, preferred_element_type=jnp.float32).astype(jnp.bfloat16)

    handed = call(
        functools.partial(asked_kernel, depth),
        shaped((half, room, width)),
        [IN_VMEM] * 2,
        [
            pltpu.VMEM((room, rows), jnp.float32),
            pltpu.VMEM((room, width), jnp.bfloat16),
            pltpu.SemaphoreType.DMA((half, 1)),
        ],
        out_space=IN_HBM,
    )(codes, item_embed)
    gathered = lax.all_to_all(
        handed, "seq", split_axis=0, concat_axis=0, tiled=True, axis_index_groups=alike
    )
    gathered = gathered.reshape(half * room, width)

    chosen = shaped((cands + slot_count, half * room))
    events = users * hist_dev
    choose_sent, choose_kept, seen = call(
        functools.partial(ready_kernel, depth, rows, hist_dev, order, handing),
        (chosen, chosen, shaped((cands, 1), jnp.int32)),
        [IN_SMEM] + [IN_VMEM] * 2,
    )(hist_lengths, codes, causal_offsets.T)

    taken = shaped((cands + slot_count, width))
    sent = call(pick_kernel, taken, [IN_VMEM] * 2)(choose_sent, gathered)
    came = lax.ppermute(sent, "seq", swap)
    kept, weight, keys, values = call(
        keep_kernel,
        (taken, shaped((width, width)), shaped((events, width)), shaped((events, width))),
        [IN_VMEM] * 2 + [IN_HBM] * 5,
        [pltpu.SemaphoreType.DMA((5,))],
    )(
        choose_kept,
        gathered,
        stay(hist_keys),
        stay(hist_values),
        stay(keys_far),
        stay(values_far),
        stay(proj_weight),
    )

    user_part, routed = call(
        attend_kernel,
        (shaped((cands, width)), shaped((cands + slot_count, width))),
        [IN_VMEM] * 6,
        [pltpu.VMEM((cands, width), jnp.bfloat16), pltpu.SemaphoreType.DMA((width // LANES,))],
        vmem=48,
        out_space=(IN_HBM, IN_VMEM),
    )(kept, came, weight, seen, keys, values)
    backs = lax.all_to_all(
        user_part.reshape(devices, slot_count, width),
        "seq",
        split_axis=0,
        concat_axis=0,
        tiled=True,
        axis_index_groups=everyone,
    )

    own_mine = lax.dynamic_slice_in_dim(routed, mine_at * slot_count, slot_count, 0)
    own_other = routed[cands:]
    routed_own = jnp.where(
        core == 0,
        jnp.concatenate([own_mine, own_other]),
        jnp.concatenate([own_other, own_mine]),
    )
    proj = jax.nn.silu(jnp.dot(routed_own, proj_weight, preferred_element_type=jnp.float32))
    gate = proj[:, :width]
    value = proj[:, width : 2 * width].astype(jnp.bfloat16)
    query = proj[:, 2 * width : 3 * width].astype(jnp.bfloat16)
    key = proj[:, 3 * width :].astype(jnp.bfloat16)
    own = self_term(query, key, value)

    cand_out = call(
        finish_kernel, shaped((slot_count, users, width)), [IN_VMEM] * 5
    )(backs, own, gate, routed_own, out_weight)
    return (item_embed, cand_out)


def solution(mesh):
    return jax.shard_map(
        per_device,
        mesh=mesh,
        in_specs=(
            P(("grp", "seq"), None),
            P(),
            P(),
            P(),
            P(),
            P("grp", "seq", None),
            P("grp", "seq", None),
            P(("grp", "seq"), None, None),
            P(("grp", "seq"), None),
            P("grp"),
            P("grp", None),
        ),
        out_specs=(P(("grp", "seq"), None), P(("grp", "seq"), None, None)),
        check_vma=False,
    )
```
